512 devices in a mesh: dp: 32 (over y, x), fsdp: 16 (over z, core).
Axes of the slice: x: 4, y: 8, z: 8, core: 2. Of those that a mesh axis runs over, the one named last changes fastest.
Arguments:
- hidden: bfloat16 [131072, 8192], P(('dp', 'fsdp')), may hold values from -6 to 6
- lengths: int32 [2048], P(('dp', 'fsdp')), may hold values from 16 to 112, as said below
- learner: int32 [2048], P(('dp', 'fsdp')), may hold values from 0 to 31, as said below
- slot_offset: int32 [2048], P(('dp', 'fsdp')), may hold values from 0 to 240, as said below
- norm_gain: bfloat16 [8192], P('fsdp'), may hold values from 0.099609375 to 1.8984375
- query_weight: bfloat16 [8192, 512], P('fsdp'), may hold values from -2 to 2
- keyval_weight: bfloat16 [8192, 256], P('fsdp'), may hold values from -2 to 2
Outputs:
- attended: bfloat16 [131072, 512], P(('dp', 'fsdp'))
The draws below stay inside these ranges and needn't reach their ends.
Inputs may be any that keep to these rules, and one draw needn't show every extreme that they name: Rows 2k and 2k+1 of one device form a pair whose lengths sum to 128; a device's rows fill its 256 slots in order. Both rows of a pair go to the same learner; every learner receives exactly 2 pairs from the devices of its fsdp index. `slot_offset`: the rows that one learner receives tile its 256 slots without gaps, in some order.
All inputs are finite; a program needn't handle non-finite values.
Results may differ from the reference program's by a relative error of at most 0.0076.
Values may be sent and summed in bfloat16 or wider, within the bound.
No kernel may reach another device: no remote copies, remote signals or barrier semaphores. Data moves between devices by JAX's collectives and lax.ppermute only.
A program may use at most 128 MiB of HBM per device.

```python
import jax
import jax.numpy as jnp
from jax import lax

D = 8192
HD = 128
QH = 4
PAIR_LEN = 128
PAIRS_DEV = 2
ROWS_DEV = 4
CAP = 256
LMIN = 16
MAX_LEN = 112
TOKENS = 131072
N_DP = 32
N_FSDP = 16


def routing_tables(key):
    lengths_key, chosen_key, pair_key, order_key = jax.random.split(jax.random.fold_in(key, 7), 4)
    lead_len = jax.random.randint(lengths_key, (N_DP, N_FSDP, PAIRS_DEV), LMIN, MAX_LEN + 1).astype(jnp.int32)
    chosen = jax.random.randint(chosen_key, (), 0, N_DP * N_FSDP * PAIRS_DEV).astype(jnp.int32)
    pair_index = jnp.arange(N_DP * N_FSDP * PAIRS_DEV, dtype=jnp.int32).reshape(N_DP, N_FSDP, PAIRS_DEV)
    lead_len = jnp.where(pair_index == chosen, LMIN, lead_len)
    pair_lengths = jnp.stack([lead_len, PAIR_LEN - lead_len], axis=-1).astype(jnp.int32)
    shuffles = jax.vmap(lambda k: jax.random.permutation(k, N_DP * PAIRS_DEV))(jax.random.split(pair_key, N_FSDP))
    slots = shuffles.astype(jnp.int32).reshape(N_FSDP, N_DP, PAIRS_DEV).transpose(1, 0, 2)
    learner_of = slots // PAIRS_DEV
    slot_index = slots % PAIRS_DEV
    local_row = slot_index[..., None] * 2 + jnp.arange(2, dtype=jnp.int32)[None, None, None, :]
    learner_full = jnp.broadcast_to(learner_of[..., None], local_row.shape)
    column_full = jnp.broadcast_to(jnp.arange(N_FSDP, dtype=jnp.int32)[None, :, None, None], local_row.shape)
    len_table = jnp.zeros((N_DP, N_FSDP, ROWS_DEV), jnp.int32).at[learner_full, column_full, local_row].set(pair_lengths)
    ranks = jax.vmap(lambda k: jax.random.permutation(k, ROWS_DEV))(jax.random.split(order_key, N_DP * N_FSDP))
    ranks = ranks.astype(jnp.int32).reshape(N_DP, N_FSDP, ROWS_DEV)
    chosen_owner = chosen // (N_FSDP * PAIRS_DEV)
    chosen_column = chosen // PAIRS_DEV % N_FSDP
    chosen_pair = chosen % PAIRS_DEV
    chosen_learner = learner_of[chosen_owner, chosen_column, chosen_pair]
    chosen_row = slot_index[chosen_owner, chosen_column, chosen_pair] * 2
    ranks = ranks.at[chosen_learner, chosen_column, chosen_row].set(ROWS_DEV)
    earlier = ranks[..., None, :] < ranks[..., :, None]
    offset_table = jnp.sum(jnp.where(earlier, len_table[..., None, :], 0), axis=-1).astype(jnp.int32)
    offsets = offset_table[learner_full, column_full, local_row]
    return (pair_lengths.reshape(-1), learner_full.reshape(-1).astype(jnp.int32), offsets.reshape(-1).astype(jnp.int32))


def draw_lengths(key, part):
    return routing_tables(key)[0]


def draw_learner(key, part):
    return routing_tables(key)[1]


def draw_slot_offset(key, part):
    return routing_tables(key)[2]


def projection_weights(key):
    query_key, fresh_key, value_key = jax.random.split(jax.random.fold_in(key, 11), 3)
    fan_scale = D ** (-0.5)
    query = jax.random.normal(query_key, (D, QH * HD), jnp.float32) * fan_scale
    value_part = jax.random.normal(value_key, (D, HD), jnp.float32) * fan_scale
    fresh = jax.random.normal(fresh_key, (D, HD), jnp.float32) * fan_scale
    key_part = fresh
    query = jnp.clip(query, -2.0, 2.0)
    both = jnp.clip(jnp.concatenate([key_part, value_part], axis=1), -2.0, 2.0)
    return (query, both)


def draw_query_weight(key, part):
    return projection_weights(key)[0].astype(jnp.bfloat16)


def draw_keyval_weight(key, part):
    return projection_weights(key)[1].astype(jnp.bfloat16)


def steps_of(key, extent, pieces, low, high):
    loudness, own = 1.0, jax.random.fold_in(key, 6)
    for dim, shards_of in pieces:
        draws = jnp.exp(jax.random.uniform(jax.random.fold_in(own, dim), (shards_of,), jnp.float32, low / len(pieces), high / len(pieces)))
        loudness = loudness * jnp.repeat(draws, extent[dim] // shards_of).reshape([-1 if axis == dim else 1 for axis in range(len(extent))])
    return loudness


def gaussian(own_key, extent, scale, limit, cuts=(), kind=jnp.bfloat16):
    factor_of = steps_of(own_key, extent, cuts, -0.22, 0.18) if cuts else 1.0
    result = jax.random.normal(own_key, extent, jnp.float32) * scale * factor_of
    return jnp.minimum(jnp.maximum(result, -limit), limit).astype(kind)


def setup_inputs(seed: int = 0) -> dict:
    seeds = jax.random.split(jax.random.key(seed), 8)
    return {
        "hidden": gaussian(seeds[0], (TOKENS, D), 1.0, 6.0, ((0, 512),)),
        "lengths": draw_lengths(jax.random.fold_in(seeds[7], 71), 0),
        "learner": draw_learner(jax.random.fold_in(seeds[7], 71), 0),
        "slot_offset": draw_slot_offset(jax.random.fold_in(seeds[7], 71), 0),
        "norm_gain": jnp.clip(1.0 + 0.18 * jax.random.normal(seeds[4], (D,), jnp.float32), 0.099609375, 1.8984375).astype(jnp.bfloat16),
        "query_weight": draw_query_weight(jax.random.fold_in(seeds[7], 71), 0),
        "keyval_weight": draw_keyval_weight(jax.random.fold_in(seeds[7], 71), 0),
    }


rope_base = 500000.0
norm_eps = 1e-05

def rotate(values, positions):
    midpoint = values.shape[-1] // 2
    frequency = rope_base ** (-jnp.arange(midpoint, dtype=jnp.float32) * 2.0 / values.shape[-1])
    angles = positions.astype(jnp.float32)[:, None] * frequency[None, :]
    cosine = jnp.cos(angles)[:, None, :]
    sines = jnp.sin(angles)[:, None, :]
    leading = values[..., :midpoint]
    trailing = values[..., midpoint:]
    return jnp.concatenate([leading * cosine - trailing * sines, trailing * cosine + leading * sines], -1)

def project_block(rows, positions, norm_gain, query_weight, keyval_weight):
    inverse = lax.rsqrt(lax.optimization_barrier(jnp.mean(jnp.square(rows.astype(jnp.float32)), axis=1, keepdims=True)) + norm_eps)
    normed = (rows.astype(jnp.float32) * inverse * norm_gain.astype(jnp.float32)[None, :]).astype(jnp.bfloat16)
    query = jnp.dot(normed, query_weight, preferred_element_type=jnp.float32)
    key_value = jnp.dot(normed, keyval_weight, preferred_element_type=jnp.float32)
    query = rotate(query.reshape(-1, QH, HD), positions).reshape(-1, QH * HD)
    key_part = rotate(key_value[:, :HD].reshape(-1, 1, HD), positions).reshape(-1, HD)
    return jnp.concatenate([query, key_part, key_value[:, HD:]], axis=1).astype(jnp.bfloat16)

def attend_block(packed, segment, position):
    query = packed[:, :QH * HD].reshape(-1, QH, HD).astype(jnp.float32)
    key_part = packed[:, QH * HD:QH * HD + HD].astype(jnp.float32)
    value_part = packed[:, QH * HD + HD:].astype(jnp.float32)
    scores = jnp.einsum('qhd,kd->hqk', query, key_part) * HD ** (-0.5)
    allowed = (segment[:, None] == segment[None, :]) & (position[None, :] <= position[:, None])
    scores = jnp.where(allowed[None], scores, -1e+30)
    row_max = lax.optimization_barrier(jnp.max(scores, axis=2, keepdims=True))
    weights = jnp.exp(scores - row_max)
    row_total = lax.optimization_barrier(jnp.sum(weights, axis=2, keepdims=True))
    probability = (weights / row_total).astype(jnp.bfloat16).astype(jnp.float32)
    mixed = jnp.einsum('hqk,kd->qhd', probability, value_part)
    return mixed.reshape(-1, QH * HD).astype(jnp.bfloat16)

def reference(hidden, lengths, learner, slot_offset, norm_gain, query_weight, keyval_weight):
    devices = N_DP * N_FSDP
    lengths_dev = lengths.reshape(devices, ROWS_DEV)
    starts = jnp.cumsum(lengths_dev, axis=1) - lengths_dev
    places = jnp.arange(CAP, dtype=jnp.int32)
    relative = places[None, :, None] - starts[:, None, :]
    inside = (relative >= 0) & (relative < lengths_dev[:, None, :])
    position = lax.optimization_barrier(jnp.sum(jnp.where(inside, relative, 0), axis=2)).astype(jnp.int32)
    row_local = lax.optimization_barrier(jnp.sum(jnp.where(inside, jnp.arange(ROWS_DEV, dtype=jnp.int32)[None, None, :], 0), axis=2)).astype(jnp.int32)
    row_global = row_local + (jnp.arange(devices, dtype=jnp.int32) * ROWS_DEV)[:, None]
    column = jnp.arange(devices, dtype=jnp.int32) % N_FSDP
    target_dev = learner.reshape(devices, ROWS_DEV) * N_FSDP + column[:, None]
    target_start = target_dev * CAP + slot_offset.reshape(devices, ROWS_DEV)
    target = jnp.take_along_axis(target_start, row_local, axis=1) + position
    source = jnp.zeros((TOKENS,), jnp.int32).at[target.reshape(-1)].set(jnp.arange(TOKENS, dtype=jnp.int32))

    def project_one(operands):
        rows, positions = operands
        return project_block(rows, positions, norm_gain, query_weight, keyval_weight)
    packed = lax.map(project_one, (hidden.reshape(devices, CAP, D), position))
    packed = packed.reshape(TOKENS, (QH + 2) * HD)[source]
    segment = row_global.reshape(-1)[source]
    learner_position = position.reshape(-1)[source]

    def attend_one(operands):
        block, seg_block, pos_block = operands
        return attend_block(block, seg_block, pos_block)
    attended = lax.map(attend_one, (packed.reshape(devices, CAP, -1), segment.reshape(devices, CAP), learner_position.reshape(devices, CAP)))
    return attended.reshape(TOKENS, QH * HD)
```

```python
import jax
import jax.numpy as jnp
from jax import lax
from jax.experimental import pallas as pl
from jax.experimental.pallas import tpu as pltpu
from jax.sharding import PartitionSpec as P

HD = 128
QH = 4
WIDE = (QH + 2) * HD
PAIR = 128

rope_base = 500000.0
norm_eps = 1e-05


def row_factors(rows, lengths):
    inverse = lax.rsqrt(
        jnp.mean(jnp.square(rows.astype(jnp.float32)), axis=1, keepdims=True) + norm_eps
    )
    lead = jnp.repeat(lengths[0::2], PAIR, total_repeat_length=rows.shape[0])
    place = jnp.arange(rows.shape[0], dtype=jnp.int32) % PAIR
    position = jnp.where(place < lead, place, place - lead)
    lane = jnp.arange(HD, dtype=jnp.int32)
    frequency = rope_base ** (-(lane % (HD // 2)).astype(jnp.float32) * 2.0 / HD)
    angles = position.astype(jnp.float32)[:, None] * frequency[None, :]
    sign = jnp.where(lane < HD // 2, -1.0, 1.0)
    return inverse, jnp.cos(angles) * inverse, jnp.sin(angles) * sign * inverse


def attend_kernel(
    lengths_ref, rows_ref, weight_ref, inverse_ref, cosine_ref, sine_ref, out_ref, total, mixed
):
    step = pl.program_id(0)
    part = jnp.dot(rows_ref[...], weight_ref[...], preferred_element_type=jnp.float32)

    @pl.when(step == 0)
    def _():
        total[...] = part

    @pl.when(step > 0)
    def _():
        total[...] += part

    @pl.when(step == pl.num_programs(0) - 1)
    def _():
        tokens = out_ref.shape[0]
        cosine, sine = cosine_ref[...], sine_ref[...]

        def rotated(head):
            values = total[:, head * HD : (head + 1) * HD]
            return (values * cosine + pltpu.roll(values, HD // 2, 1) * sine).astype(jnp.bfloat16)

        heads = [rotated(h) for h in range(QH)]
        key_part = rotated(QH)
        value_part = (total[:, (QH + 1) * HD :] * inverse_ref[...]).astype(jnp.bfloat16)
        asks = lax.broadcasted_iota(jnp.int32, (PAIR, PAIR), 0)
        keys = lax.broadcasted_iota(jnp.int32, (PAIR, PAIR), 1)
        for pair in range(tokens // PAIR):
            own = slice(pair * PAIR, (pair + 1) * PAIR)
            lead = lengths_ref[2 * pair]
            allowed = (keys <= asks) & ((asks < lead) | (keys >= lead))
            allowed = jnp.concatenate([allowed.astype(jnp.int32)] * QH, axis=0) > 0
            query = jnp.concatenate([h[own] for h in heads], axis=0)
            scores = lax.dot_general(
                query, key_part[own], (((1,), (1,)), ((), ())), preferred_element_type=jnp.float32
            ) * (HD**-0.5)
            scores = jnp.where(allowed, scores, -1e30)
            weights = jnp.exp(scores - jnp.max(scores, axis=1, keepdims=True))
            probability = (weights / jnp.sum(weights, axis=1, keepdims=True)).astype(jnp.bfloat16)
            result = jnp.dot(
                probability, value_part[own], preferred_element_type=jnp.float32
            ).astype(jnp.bfloat16)
            for h in range(QH):
                mixed[own, h * HD : (h + 1) * HD] = result[h * PAIR : (h + 1) * PAIR]
        row = lax.broadcasted_iota(jnp.int32, (tokens, tokens), 0)
        token = lax.broadcasted_iota(jnp.int32, (tokens, tokens), 1)
        source = ((row >> 2) & 1) * PAIR + (row >> 3) * 4 + (row & 3)
        order = jnp.where(token == source, 1.0, 0.0).astype(jnp.bfloat16)
        out_ref[...] = jnp.dot(order, mixed[...], preferred_element_type=jnp.float32).astype(
            out_ref.dtype
        )


def attend(rows, lengths, weight, inverse, cosine, sine):
    tokens, depth = rows.shape
    block = 1024
    return pl.pallas_call(
        attend_kernel,
        out_shape=jax.ShapeDtypeStruct((tokens, QH * HD), jnp.bfloat16),
        grid=(depth // block,),
        in_specs=[
            pl.BlockSpec(memory_space=pltpu.SMEM),
            pl.BlockSpec((tokens, block), lambda k: (0, k)),
            pl.BlockSpec((block, WIDE), lambda k: (k, 0)),
            pl.BlockSpec((tokens, 1), lambda k: (0, 0)),
            pl.BlockSpec((tokens, HD), lambda k: (0, 0)),
            pl.BlockSpec((tokens, HD), lambda k: (0, 0)),
        ],
        out_specs=pl.BlockSpec((tokens, QH * HD), lambda k: (0, 0)),
        scratch_shapes=[
            pltpu.VMEM((tokens, WIDE), jnp.float32),
            pltpu.VMEM((tokens, QH * HD), jnp.bfloat16),
        ],
        compiler_params=pltpu.CompilerParams(vmem_limit_bytes=24 << 20),
        cost_estimate=pl.CostEstimate(
            flops=2 * tokens * depth * WIDE, bytes_accessed=2 * depth * (tokens + WIDE), transcendentals=0
        ),
    )(lengths, rows, weight, inverse, cosine, sine)


def routes(lengths, learner, slot_offset):
    table = jnp.concatenate([lengths, learner, slot_offset]).reshape(3, -1)
    table = lax.all_gather(table, "dp", axis=0).transpose(1, 0, 2).reshape(3, -1, 2)
    lead, target, offset = table[0, :, 0], table[1, :, 0], table[2]
    pairs = target.shape[0]
    number = jnp.arange(pairs, dtype=jnp.int32)
    before = (target[None, :] < target[:, None]) | (
        (target[None, :] == target[:, None]) & (number[None, :] < number[:, None])
    )
    rank = jnp.sum(before.astype(jnp.int32), axis=1)
    rows = 4 * pairs
    row = jnp.arange(rows, dtype=jnp.int32)
    goes = jnp.repeat(rank, 4, total_repeat_length=rows) * 4 + row % 4
    first = (row[:, None] == goes[None, :]).astype(jnp.bfloat16)
    kept = (row // 4) % 2
    mine = (rank[None, :] == (2 * lax.axis_index("dp") + kept)[:, None]).astype(jnp.int32)
    own_lead = jnp.sum(mine * lead[None, :], axis=1)
    own_first = jnp.sum(mine * offset[None, :, 0], axis=1)
    own_second = jnp.sum(mine * offset[None, :, 1], axis=1)
    token = (row // 8) * 4 + row % 4
    slot = jnp.where(token < own_lead, own_first + token, own_second + token - own_lead)
    last = (row[:, None] == slot[None, :]).astype(jnp.bfloat16)
    return first, last


def exchange(rows):
    peers = lax.axis_size("dp")
    blocks = rows.reshape(peers, -1, rows.shape[1])
    return lax.all_to_all(blocks, "dp", split_axis=0, concat_axis=0, tiled=True).reshape(rows.shape)


def shards(hidden, lengths, learner, slot_offset, norm_gain, query_weight, keyval_weight):
    scaled = norm_gain.astype(jnp.float32)[:, None] * jnp.concatenate(
        [query_weight, keyval_weight], axis=1
    ).astype(jnp.float32)
    weight = lax.all_gather(scaled.astype(jnp.bfloat16), "fsdp", axis=0, tiled=True)
    first, last = routes(lengths, learner, slot_offset)
    inverse, cosine, sine = row_factors(hidden, lengths)
    mixed = attend(hidden, lengths, weight, inverse, cosine, sine)
    spread = exchange(mixed)
    arranged = jnp.dot(first, spread, preferred_element_type=jnp.float32).astype(jnp.bfloat16)
    landed = exchange(arranged)
    return jnp.dot(last, landed, preferred_element_type=jnp.float32).astype(jnp.bfloat16)


def solution(mesh):
    placed = (
        P(("dp", "fsdp"), None),
        P(("dp", "fsdp")),
        P(("dp", "fsdp")),
        P(("dp", "fsdp")),
        P("fsdp"),
        P("fsdp", None),
        P("fsdp", None),
    )
    return jax.shard_map(
        shards, mesh=mesh, in_specs=placed, out_specs=P(("dp", "fsdp"), None), check_vma=False
    )
```

```python
import jax
import jax.numpy as jnp
from jax import lax
from jax.experimental import pallas as pl
from jax.experimental.pallas import tpu as pltpu
from jax.sharding import PartitionSpec as P

HD = 128
QH = 4
WIDE = (QH + 2) * HD
PAIR = 128

rope_base = 500000.0
norm_eps = 1e-05

f32 = jnp.float32
bf16 = jnp.bfloat16


def whole(shape):
    return pl.BlockSpec(shape, lambda *_: (0,) * len(shape))


def fold_kernel(gain_ref, query_ref, keyval_ref, *out_refs):
    depth = query_ref.shape[0]
    row = lax.broadcasted_iota(jnp.int32, (depth, depth), 0)
    column = lax.broadcasted_iota(jnp.int32, (depth, depth), 1)
    gain = jnp.where(row == column, gain_ref[...].astype(f32), 0.0).astype(bf16)
    query = jnp.dot(gain, query_ref[...], preferred_element_type=f32).astype(bf16)
    keyval = jnp.dot(gain, keyval_ref[...], preferred_element_type=f32).astype(bf16)
    rows = out_refs[0].shape[0]
    for i, out_ref in enumerate(out_refs):
        out_ref[:, : QH * HD] = query[i * rows : (i + 1) * rows]
        out_ref[:, QH * HD :] = keyval[i * rows : (i + 1) * rows]


def fold(gain, query_weight, keyval_weight):
    depth = gain.shape[0]
    half = jax.ShapeDtypeStruct((depth // 2, WIDE), bf16)
    return pl.pallas_call(fold_kernel, out_shape=(half, half), name="fold_gain")(
        gain.reshape(1, depth), query_weight, keyval_weight
    )


def prepare_kernel(where_ref, keep_ref, give_ref, out_ref, inverse_ref, squares):
    step = pl.program_id(0)
    out_ref[...] = give_ref[...]
    both = jnp.square(keep_ref[...].astype(f32)) + jnp.square(give_ref[...].astype(f32))
    part = sum(both[:, i * 128 : (i + 1) * 128] for i in range(both.shape[1] // 128))

    @pl.when(step == 0)
    def _():
        squares[...] = part

    @pl.when(step > 0)
    def _():
        squares[...] += part

    @pl.when(step == pl.num_programs(0) - 1)
    def _():
        depth = 2 * pl.num_programs(0) * keep_ref.shape[1]
        mean = jnp.sum(squares[...], axis=1, keepdims=True) / depth
        inverse_ref[...] = jnp.broadcast_to(lax.rsqrt(mean + norm_eps), inverse_ref.shape)


def prepare(rows, where, block):
    tokens, depth = rows.shape
    steps = depth // (2 * block)
    return pl.pallas_call(
        prepare_kernel,
        out_shape=(
            jax.ShapeDtypeStruct((tokens, depth // 2), bf16),
            jax.ShapeDtypeStruct((tokens, HD), f32),
        ),
        grid_spec=pltpu.PrefetchScalarGridSpec(
            num_scalar_prefetch=1,
            grid=(steps,),
            in_specs=[
                pl.BlockSpec((tokens, block), lambda i, where: (0, 2 * i + where[1])),
                pl.BlockSpec((tokens, block), lambda i, where: (0, 2 * i + 1 - where[1])),
            ],
            out_specs=[
                pl.BlockSpec((tokens, block), lambda i, where: (0, i)),
                pl.BlockSpec((tokens, HD), lambda i, where: (0, 0)),
            ],
            scratch_shapes=[pltpu.VMEM((tokens, 128), f32)],
        ),
        cost_estimate=pl.CostEstimate(
            flops=3 * tokens * depth, bytes_accessed=3 * tokens * depth, transcendentals=0
        ),
        name="prepare",
    )(where, rows, rows)


def partial_kernel(count, carried, place_ref, *refs):
    weights, columns = refs[:count], refs[count : 2 * count]
    out_ref = refs[-1]
    total = jnp.dot(columns[0][...], weights[0][...], preferred_element_type=f32)
    for c, w in zip(columns[1:], weights[1:]):
        total += jnp.dot(c[...], w[...], preferred_element_type=f32)
    out_ref[...] = refs[2 * count][...] + total if carried else total


def partial(rows, where, blocks, before, ring, shared):
    count, tokens = len(blocks), rows.shape[0]
    weights = [w for _, _, w in blocks]
    depth = weights[0].shape[0]
    carried = before is not None

    def columns(distance, half):
        def index(_, where):
            place = lax.rem(where[0] + (distance + ring), ring)
            return 0, (4 * place + 2 * where[1] + half if shared else 2 * place + half)

        return pl.BlockSpec((tokens, depth), index)

    total = whole((tokens, WIDE))
    return pl.pallas_call(
        lambda *refs: partial_kernel(count, carried, *refs),
        out_shape=jax.ShapeDtypeStruct((tokens, WIDE), f32),
        grid_spec=pltpu.PrefetchScalarGridSpec(
            num_scalar_prefetch=1,
            grid=(1,),
            in_specs=[whole((depth, WIDE))] * count
            + [columns(d, h) for d, h, _ in blocks]
            + [total] * carried,
            out_specs=total,
        ),
        compiler_params=pltpu.CompilerParams(vmem_limit_bytes=24 << 20),
        cost_estimate=pl.CostEstimate(
            flops=2 * tokens * depth * WIDE * count,
            bytes_accessed=2 * depth * (tokens + WIDE) * count + 4 * tokens * WIDE * (1 + carried),
            transcendentals=0,
        ),
        name="partial_sums",
    )(where, *weights, *[rows] * count, *([before] if carried else []))


def attend_kernel(lengths_ref, mine_ref, other_ref, inverse_ref, cosine_ref, sine_ref, out_ref, mixed):
    tokens = out_ref.shape[0]
    inverse = inverse_ref[...]
    cosine, sine = cosine_ref[...] * inverse, sine_ref[...] * inverse

    def product(head):
        own = slice(head * HD, (head + 1) * HD)
        return mine_ref[:, own] + other_ref[:, own]

    def rotated(head):
        values = product(head)
        return (values * cosine + pltpu.roll(values, HD // 2, 1) * sine).astype(bf16)

    heads = [rotated(h) for h in range(QH)]
    key_part = rotated(QH)
    value_part = (product(QH + 1) * inverse).astype(bf16)
    asks = lax.broadcasted_iota(jnp.int32, (PAIR, PAIR), 0)
    keys = lax.broadcasted_iota(jnp.int32, (PAIR, PAIR), 1)
    for pair in range(tokens // PAIR):
        own = slice(pair * PAIR, (pair + 1) * PAIR)
        lead = lengths_ref[2 * pair]
        allowed = (keys <= asks) & ((asks < lead) | (keys >= lead))
        allowed = jnp.concatenate([allowed.astype(jnp.int32)] * QH, axis=0) > 0
        query = jnp.concatenate([h[own] for h in heads], axis=0)
        scores = lax.dot_general(
            query, key_part[own], (((1,), (1,)), ((), ())), preferred_element_type=f32
        ) * (HD**-0.5)
        scores = jnp.where(allowed, scores, -1e30)
        weights = jnp.exp(scores - jnp.max(scores, axis=1, keepdims=True))
        probability = (weights / jnp.sum(weights, axis=1, keepdims=True)).astype(bf16)
        result = jnp.dot(probability, value_part[own], preferred_element_type=f32).astype(bf16)
        for h in range(QH):
            mixed[own, h * HD : (h + 1) * HD] = result[h * PAIR : (h + 1) * PAIR]
    row = lax.broadcasted_iota(jnp.int32, (tokens, tokens), 0)
    token = lax.broadcasted_iota(jnp.int32, (tokens, tokens), 1)
    source = ((row >> 2) & 1) * PAIR + (row >> 3) * 4 + (row & 3)
    order = jnp.where(token == source, 1.0, 0.0).astype(bf16)
    out_ref[...] = jnp.dot(order, mixed[...], preferred_element_type=f32).astype(out_ref.dtype)


def attend(lengths, mine, other, inverse, cosine, sine):
    tokens = mine.shape[0]
    vmem = pl.BlockSpec(memory_space=pltpu.VMEM)
    return pl.pallas_call(
        attend_kernel,
        out_shape=jax.ShapeDtypeStruct((tokens, QH * HD), bf16),
        in_specs=[pl.BlockSpec(memory_space=pltpu.SMEM)] + [vmem] * 5,
        out_specs=vmem,
        scratch_shapes=[pltpu.VMEM((tokens, QH * HD), bf16)],
        name="attend",
    )(lengths, mine, other, inverse, cosine, sine)


def rotary(lengths, tokens):
    slot = jnp.arange(tokens, dtype=jnp.int32)
    place = slot % PAIR
    lead = sum(jnp.where(slot // PAIR == k, lengths[2 * k], 0) for k in range(tokens // PAIR))
    position = jnp.where(place < lead, place, place - lead)
    lane = jnp.arange(HD, dtype=jnp.int32)
    frequency = rope_base ** (-(lane % (HD // 2)).astype(f32) * 2.0 / HD)
    angles = position.astype(f32)[:, None] * frequency[None, :]
    sign = jnp.where(lane < HD // 2, -1.0, 1.0)
    return jnp.cos(angles), jnp.sin(angles) * sign


def orders_kernel(me_ref, table_ref, first_ref, last_ref):
    rows = first_ref.shape[0]
    peers = table_ref.shape[0]
    down = lax.broadcasted_iota(jnp.int32, (rows, rows), 0)
    along = lax.broadcasted_iota(jnp.int32, (rows, rows), 1)
    table = table_ref[:, 0, :].astype(f32).astype(bf16)
    spread = jnp.where(
        lax.broadcasted_iota(jnp.int32, (rows, peers), 1)
        == lax.broadcasted_iota(jnp.int32, (rows, peers), 0) // 8,
        1.0,
        0.0,
    ).astype(bf16)
    table = jnp.dot(spread, table, preferred_element_type=f32)
    place = lax.broadcasted_iota(jnp.int32, (rows, 1), 0)
    second = (place // 4) % 2 == 1

    def pick(even, odd):
        return jnp.where(second, table[:, odd : odd + 1], table[:, even : even + 1])

    lead, target = pick(0, 2), pick(4, 6)
    offset_a, offset_b = pick(8, 10), pick(9, 11)
    key = target * rows + (place // 4).astype(f32)
    key_along = jnp.sum(jnp.where(down == along, key, 0.0), axis=0, keepdims=True)
    ahead_along = jnp.sum(jnp.where(key < key_along, 1.0, 0.0), axis=0, keepdims=True)
    ahead = jnp.sum(jnp.where(key_along < key, 1.0, 0.0), axis=1, keepdims=True)
    row = lax.broadcasted_iota(jnp.int32, (1, rows), 1)
    goes = ahead_along.astype(jnp.int32) + row % 4
    first_ref[...] = jnp.where(down == goes, 1.0, 0.0).astype(bf16)
    token = (row // 8) * 4 + row % 4

    def slots(k):
        mine = (ahead.astype(jnp.int32) == 4 * (2 * me_ref[0] + k)) & (place % 4 == 0)

        def own(values):
            return jnp.sum(jnp.where(mine, values, 0.0), axis=0, keepdims=True).astype(jnp.int32)

        return jnp.where(
            token < own(lead), own(offset_a) + token, own(offset_b) + token - own(lead)
        )

    slot = jnp.where((row // 4) % 2 == 0, slots(0), slots(1))
    last_ref[...] = jnp.where(down == slot, 1.0, 0.0).astype(bf16)


def orders(table, rows):
    order = jax.ShapeDtypeStruct((rows, rows), bf16)
    vmem = pl.BlockSpec(memory_space=pltpu.VMEM)
    return pl.pallas_call(
        orders_kernel,
        out_shape=(order, order),
        in_specs=[pl.BlockSpec(memory_space=pltpu.SMEM), vmem],
        out_specs=(vmem, vmem),
        name="row_orders",
    )(lax.axis_index("dp").reshape(1), table)


def to_peers(blocks):
    return lax.all_to_all(blocks, "dp", split_axis=0, concat_axis=0, tiled=True)


def exchange(rows):
    return to_peers(rows.reshape(lax.axis_size("dp"), -1, rows.shape[1])).reshape(rows.shape)


def shards(hidden, lengths, learner, slot_offset, norm_gain, query_weight, keyval_weight):
    tokens = hidden.shape[0]
    block = norm_gain.shape[0]
    size = lax.axis_size("fsdp")
    ring = size // 2
    index = lax.axis_index("fsdp")
    where = jnp.stack([index // 2, index % 2])
    up = [(i, (i + 2) % size) for i in range(size)]
    down = [(i, (i - 2) % size) for i in range(size)]
    swap = [(i, i ^ 1) for i in range(size)]

    def send(values, pairs):
        return lax.ppermute(values, "fsdp", pairs)

    def after(value, *others):
        return lax.optimization_barrier((value, *others))[0]

    held = fold(norm_gain, query_weight, keyval_weight)
    give, inverse = prepare(hidden, after(where, held[0]), block)
    got = send(give, swap)

    def add(blocks, before, side):
        return partial((hidden, got)[side], where, blocks, before, ring, side == 0)

    above, below = list(held), list(held)
    sums = [None, None]
    blocks = [(0, h, held[h]) for h in (0, 1)]
    for step in range(1, ring // 2):
        above = [send(w, up) for w in above]
        below = [send(w, down) for w in below]
        sums = [add(blocks, before, side) for side, before in enumerate(sums)]
        wanted = list(sums)
        if step == 1:
            table = jnp.pad(jnp.concatenate([lengths, learner, slot_offset]), (0, 116))
            table = jnp.broadcast_to(after(table, above[0]), (lax.axis_size("dp"), 8, 128))
            first, last = orders(to_peers(table), tokens)
            cosine, sine = rotary(after(lengths, above[0]), tokens)
        if step == 2:
            wanted += [first, last, cosine, sine]
        above[0] = after(above[0], *wanted)
        blocks = [(-step, h, above[h]) for h in (0, 1)] + [(step, h, below[h]) for h in (0, 1)]
    far = [(ring // 2, 0, send(above[0], up)), (ring // 2, 1, send(below[1], down))]
    sums = [add(blocks, before, side) for side, before in enumerate(sums)]
    far[1] = (*far[1][:2], after(far[1][2], *sums))
    other = send(add(far, sums[1], 1), swap)
    mine = add(far, sums[0], 0)
    mixed = attend(lengths, mine, other, inverse, cosine, sine)
    spread = exchange(mixed)
    arranged = jnp.dot(first, spread, preferred_element_type=f32).astype(bf16)
    landed = exchange(arranged)
    return jnp.dot(last, landed, preferred_element_type=f32).astype(bf16)


def solution(mesh):
    placed = (
        P(("dp", "fsdp"), None),
        P(("dp", "fsdp")),
        P(("dp", "fsdp")),
        P(("dp", "fsdp")),
        P("fsdp"),
        P("fsdp", None),
        P("fsdp", None),
    )
    return jax.shard_map(
        shards, mesh=mesh, in_specs=placed, out_specs=P(("dp", "fsdp"), None), check_vma=False
    )
```

```python
import functools

import jax
import jax.numpy as jnp
from jax import lax
from jax.experimental import pallas as pl
from jax.experimental.pallas import tpu as pltpu
from jax.sharding import PartitionSpec as P

HD = 128
QH = 4
WIDE = (QH + 2) * HD
PAIR = 128
TABLE = 128

rope_base = 500000.0
norm_eps = 1e-05

f32 = jnp.float32
bf16 = jnp.bfloat16


VMEM = pl.BlockSpec(memory_space=pltpu.VMEM)
SMEM = pl.BlockSpec(memory_space=pltpu.SMEM)


def fold_kernel(gain_ref, query_ref, keyval_ref, *out_refs):
    rows = out_refs[0].shape[0]
    row = lax.broadcasted_iota(jnp.int32, (rows, rows), 0)
    column = lax.broadcasted_iota(jnp.int32, (rows, rows), 1)
    for i, out_ref in enumerate(out_refs):
        own = slice(i * rows, (i + 1) * rows)
        gain = gain_ref[own].astype(f32).reshape(1, rows)
        gain = jnp.where(row == column, gain, 0.0).astype(bf16)
        out_ref[:, : QH * HD] = jnp.dot(gain, query_ref[own, :], preferred_element_type=f32).astype(bf16)
        out_ref[:, QH * HD :] = jnp.dot(gain, keyval_ref[own, :], preferred_element_type=f32).astype(bf16)


def fold(gain, query_weight, keyval_weight):
    half = jax.ShapeDtypeStruct((gain.shape[0] // 2, WIDE), bf16)
    return pl.pallas_call(
        fold_kernel,
        out_shape=(half, half),
        in_specs=[VMEM] * 3,
        out_specs=(VMEM, VMEM),
        name="fold_gain",
    )(gain, query_weight, keyval_weight)


def prepare_kernel(where_ref, keep_ref, give_ref, out_ref, inverse_ref, squares):
    step = pl.program_id(0)
    out_ref[...] = give_ref[...]
    part = jnp.zeros(squares.shape, f32)
    for i in range(keep_ref.shape[1] // 128):
        for ref in (keep_ref, give_ref):
            part += jnp.square(ref[:, i * 128 : (i + 1) * 128].astype(f32))

    @pl.when(step == 0)
    def _():
        squares[...] = part

    @pl.when(step > 0)
    def _():
        squares[...] += part

    @pl.when(step == pl.num_programs(0) - 1)
    def _():
        depth = 2 * pl.num_programs(0) * keep_ref.shape[1]
        mean = jnp.sum(squares[...], axis=1, keepdims=True) / depth
        inverse_ref[...] = jnp.broadcast_to(lax.rsqrt(mean + norm_eps), inverse_ref.shape)


def prepare(rows, where, block):
    tokens, depth = rows.shape
    steps = depth // (2 * block)
    return pl.pallas_call(
        prepare_kernel,
        out_shape=(
            jax.ShapeDtypeStruct((tokens, depth // 2), bf16),
            jax.ShapeDtypeStruct((tokens, HD), f32),
        ),
        grid_spec=pltpu.PrefetchScalarGridSpec(
            num_scalar_prefetch=1,
            grid=(steps,),
            in_specs=[
                pl.BlockSpec((tokens, block), lambda i, where: (0, 2 * i + where[1])),
                pl.BlockSpec((tokens, block), lambda i, where: (0, 2 * i + 1 - where[1])),
            ],
            out_specs=[
                pl.BlockSpec((tokens, block), lambda i, where: (0, i)),
                pl.BlockSpec((tokens, HD), lambda i, where: (0, 0)),
            ],
            scratch_shapes=[pltpu.VMEM((tokens, 128), f32)],
        ),
        cost_estimate=pl.CostEstimate(
            flops=3 * tokens * depth, bytes_accessed=3 * tokens * depth, transcendentals=0
        ),
        name="prepare",
    )(where, rows, rows)


def partial_kernel(count, sides, carried, where_ref, *refs):
    weights, refs = refs[:count], refs[count:]
    columns, refs = refs[: count * sides], refs[count * sides :]
    for side in range(sides):
        total = refs[side][...] if carried else None
        for c, w in zip(columns[side * count :], weights):
            part = jnp.dot(c[...], w[...], preferred_element_type=f32)
            total = part if total is None else total + part
        refs[-sides + side][...] = total


def partial(where, blocks, rows, before):
    count, sides = len(blocks), len(rows)
    weights = [w for _, _, w in blocks]
    tokens, depth = rows[0].shape[0], weights[0].shape[0]
    ring = lax.axis_size("fsdp") // 2
    carried = before is not None

    def columns(distance, half, shared):
        def index(_, where):
            origin = lax.rem(where[0] + ring + (2 * where[1] - 1) * distance, ring)
            return 0, (4 * origin + 2 * where[1] + half if shared else 2 * origin + half)

        return pl.BlockSpec((tokens, depth), index)

    total = pl.BlockSpec((tokens, WIDE), lambda *_: (0, 0))
    shape = jax.ShapeDtypeStruct((tokens, WIDE), f32)
    return pl.pallas_call(
        functools.partial(partial_kernel, count, sides, carried),
        out_shape=[shape] * sides,
        grid_spec=pltpu.PrefetchScalarGridSpec(
            num_scalar_prefetch=1,
            grid=(1,),
            in_specs=[pl.BlockSpec((depth, WIDE), lambda *_: (0, 0))] * count
            + [columns(d, h, r.shape[1] == 4 * ring * depth) for r in rows for d, h, _ in blocks]
            + [total] * (sides * carried),
            out_specs=[total] * sides,
        ),
        compiler_params=pltpu.CompilerParams(vmem_limit_bytes=28 << 20),
        cost_estimate=pl.CostEstimate(
            flops=2 * tokens * depth * WIDE * count * sides,
            bytes_accessed=2 * depth * (sides * tokens + WIDE) * count + 8 * tokens * WIDE * sides,
            transcendentals=0,
        ),
        name="partial_sums",
    )(where, *weights, *[r for r in rows for _ in blocks], *(before or []))


def attend_kernel(
    lengths_ref, learner_ref, offset_ref, mine_ref, other_ref, inverse_ref, cosine_ref, sine_ref, out_ref, mixed
):
    tokens = out_ref.shape[0]
    inverse = inverse_ref[...]
    cosine, sine = cosine_ref[...] * inverse, sine_ref[...] * inverse

    def product(head):
        own = slice(head * HD, (head + 1) * HD)
        return mine_ref[:, own] + other_ref[:, own]

    def rotated(head):
        values = product(head)
        return (values * cosine + pltpu.roll(values, HD // 2, 1) * sine).astype(bf16)

    heads = [rotated(h) for h in range(QH)]
    key_part = rotated(QH)
    value_part = (product(QH + 1) * inverse).astype(bf16)
    asks = lax.broadcasted_iota(jnp.int32, (PAIR, PAIR), 0)
    keys = lax.broadcasted_iota(jnp.int32, (PAIR, PAIR), 1)
    for pair in range(tokens // PAIR):
        own = slice(pair * PAIR, (pair + 1) * PAIR)
        lead = lengths_ref[2 * pair]
        allowed = (keys <= asks) & ((asks < lead) | (keys >= lead))
        allowed = jnp.concatenate([allowed.astype(jnp.int32)] * QH, axis=0) > 0
        query = jnp.concatenate([h[own] for h in heads], axis=0)
        scores = lax.dot_general(
            query, key_part[own], (((1,), (1,)), ((), ())), preferred_element_type=f32
        ) * (HD**-0.5)
        scores = jnp.where(allowed, scores, -1e30)
        weights = jnp.exp(scores - jnp.max(scores, axis=1, keepdims=True))
        probability = (weights / jnp.sum(weights, axis=1, keepdims=True)).astype(bf16)
        result = jnp.dot(probability, value_part[own], preferred_element_type=f32).astype(bf16)
        for h in range(QH):
            mixed[own, h * HD : (h + 1) * HD] = result[h * PAIR : (h + 1) * PAIR]
    row = lax.broadcasted_iota(jnp.int32, (tokens, tokens), 0)
    token = lax.broadcasted_iota(jnp.int32, (tokens, tokens), 1)
    source = ((row >> 2) & 1) * PAIR + (row >> 3) * 4 + (row & 3)
    order = jnp.where(token == source, 1.0, 0.0).astype(bf16)
    out_ref[:, : QH * HD] = jnp.dot(order, mixed[...], preferred_element_type=f32).astype(bf16)
    lane = lax.broadcasted_iota(jnp.int32, (tokens, TABLE), 1)
    table = jnp.zeros((tokens, TABLE), jnp.int32)
    for i, ref in enumerate((lengths_ref, learner_ref, offset_ref)):
        for j in range(4):
            table = jnp.where(lane == 4 * i + j, ref[j], table)
    out_ref[:, QH * HD :] = table.astype(f32).astype(bf16)


def attend(lengths, learner, slot_offset, mine, other, inverse, cosine, sine):
    tokens = mine.shape[0]
    return pl.pallas_call(
        attend_kernel,
        out_shape=jax.ShapeDtypeStruct((tokens, QH * HD + TABLE), bf16),
        in_specs=[SMEM] * 3 + [VMEM] * 5,
        out_specs=VMEM,
        scratch_shapes=[pltpu.VMEM((tokens, QH * HD), bf16)],
        name="attend",
    )(lengths, learner, slot_offset, mine, other, inverse, cosine, sine)


def rotary(lengths, tokens):
    slot = jnp.arange(tokens, dtype=jnp.int32)
    place = slot % PAIR
    lead = sum(jnp.where(slot // PAIR == k, lengths[2 * k], 0) for k in range(tokens // PAIR))
    position = jnp.where(place < lead, place, place - lead)
    lane = jnp.arange(HD, dtype=jnp.int32)
    frequency = rope_base ** (-(lane % (HD // 2)).astype(f32) * 2.0 / HD)
    angles = position.astype(f32)[:, None] * frequency[None, :]
    sign = jnp.where(lane < HD // 2, -1.0, 1.0)
    return jnp.cos(angles), jnp.sin(angles) * sign


def ranks(spread_ref):
    rows = spread_ref.shape[0]
    place = lax.broadcasted_iota(jnp.int32, (rows, 1), 0)
    table = spread_ref[:, QH * HD :].astype(f32)
    target = jnp.where((place // 4) % 2 == 1, table[:, 6:7], table[:, 4:5])
    key = target * rows + (place // 4).astype(f32)
    down = lax.broadcasted_iota(jnp.int32, (rows, rows), 0)
    along = lax.broadcasted_iota(jnp.int32, (rows, rows), 1)
    key_along = jnp.sum(jnp.where(down == along, key, 0.0), axis=0, keepdims=True)
    ahead_along = jnp.sum(jnp.where(key < key_along, 1.0, 0.0), axis=0, keepdims=True)
    return table, place, key, key_along, ahead_along.astype(jnp.int32), down


def arrange_kernel(spread_ref, out_ref):
    *_, ahead_along, down = ranks(spread_ref)
    row = lax.broadcasted_iota(jnp.int32, ahead_along.shape, 1)
    order = jnp.where(down == ahead_along + row % 4, 1.0, 0.0).astype(bf16)
    out_ref[...] = jnp.dot(order, spread_ref[:, : QH * HD], preferred_element_type=f32).astype(bf16)


def slots_kernel(me_ref, spread_ref, out_ref):
    table, place, key, key_along, _, down = ranks(spread_ref)
    ahead = jnp.sum(jnp.where(key_along < key, 1.0, 0.0), axis=1, keepdims=True).astype(jnp.int32)
    second = (place // 4) % 2 == 1
    row = lax.broadcasted_iota(jnp.int32, key_along.shape, 1)
    token = (row // 8) * 4 + row % 4

    def slots(k):
        mine = (ahead == 4 * (2 * me_ref[0] + k)) & (place % 4 == 0)

        def own(even, odd):
            values = jnp.where(second, table[:, odd : odd + 1], table[:, even : even + 1])
            return jnp.sum(jnp.where(mine, values, 0.0), axis=0, keepdims=True).astype(jnp.int32)

        lead = own(0, 2)
        return jnp.where(token < lead, own(8, 10) + token, own(9, 11) + token - lead)

    slot = jnp.where((row // 4) % 2 == 0, slots(0), slots(1))
    out_ref[...] = jnp.where(down == slot, 1.0, 0.0).astype(bf16)


def arrange(spread):
    return pl.pallas_call(
        arrange_kernel,
        out_shape=jax.ShapeDtypeStruct((spread.shape[0], QH * HD), bf16),
        in_specs=[VMEM],
        out_specs=VMEM,
        name="arrange",
    )(spread)


def slots(spread):
    return pl.pallas_call(
        slots_kernel,
        out_shape=jax.ShapeDtypeStruct((spread.shape[0],) * 2, bf16),
        in_specs=[SMEM, VMEM],
        out_specs=VMEM,
        name="slots",
    )(lax.axis_index("dp").reshape(1), spread)


def exchange(rows):
    blocks = rows.reshape(lax.axis_size("dp"), -1, rows.shape[1])
    return lax.all_to_all(blocks, "dp", split_axis=0, concat_axis=0, tiled=True).reshape(rows.shape)


def shards(hidden, lengths, learner, slot_offset, norm_gain, query_weight, keyval_weight):
    tokens = hidden.shape[0]
    block = norm_gain.shape[0]
    size = lax.axis_size("fsdp")
    ring = size // 2
    index = lax.axis_index("fsdp")
    onward = [(i, (i + 2 - 4 * (i % 2)) % size) for i in range(size)]
    swap = [(i, i ^ 1) for i in range(size)]

    def send(values, pairs):
        return lax.ppermute(values, "fsdp", pairs)

    def after(value, *others):
        return lax.optimization_barrier((value, *others))[0]

    where = jnp.stack([index // 2, index % 2])
    moving = list(fold(norm_gain, query_weight, keyval_weight))
    blocks = [(0, h, moving[h]) for h in (0, 1)]
    sums = None
    for step in range(1, ring):
        moving = [send(w, onward) for w in moving]
        if step == 1:
            give, inverse = prepare(hidden, after(where, *moving), block)
            got = send(give, swap)
            cosine, sine = rotary(after(lengths, *moving), tokens)
        if step in (3, 5, ring - 1):
            sums = partial(where, blocks, (hidden, got), sums)
            blocks = []
            moving[0] = after(moving[0], *sums)
        if step == 4:
            moving[0] = after(moving[0], inverse, cosine, sine)
        blocks += [(step, h, moving[h]) for h in (0, 1)]
    [other] = partial(where, blocks, (got,), sums[1:])
    other = send(other, swap)
    [mine] = partial(where, blocks, (hidden,), sums[:1])
    mixed = attend(lengths, learner, slot_offset, mine, other, inverse, cosine, sine)
    spread = exchange(mixed)
    landed = exchange(arrange(spread))
    return jnp.dot(slots(spread), landed, preferred_element_type=f32).astype(bf16)


def solution(mesh):
    placed = (
        P(("dp", "fsdp"), None),
        P(("dp", "fsdp")),
        P(("dp", "fsdp")),
        P(("dp", "fsdp")),
        P("fsdp"),
        P("fsdp", None),
        P("fsdp", None),
    )
    return jax.shard_map(
        shards, mesh=mesh, in_specs=placed, out_specs=P(("dp", "fsdp"), None), check_vma=False
    )
```

```python
import functools

import jax
import jax.numpy as jnp
from jax import lax
from jax.experimental import pallas as pl
from jax.experimental.pallas import tpu as pltpu
from jax.sharding import PartitionSpec as P

HD = 128
QH = 4
WIDE = (QH + 2) * HD
PAIR = 128
TABLE = 128
PIECE = 256

rope_base = 500000.0
norm_eps = 1e-05

f32 = jnp.float32
bf16 = jnp.bfloat16


VMEM = pl.BlockSpec(memory_space=pltpu.VMEM)
SMEM = pl.BlockSpec(memory_space=pltpu.SMEM)


def fold_kernel(gain_ref, query_ref, keyval_ref, *out_refs):
    rows = 256
    row = lax.broadcasted_iota(jnp.int32, (rows, rows), 0)
    column = lax.broadcasted_iota(jnp.int32, (rows, rows), 1)
    for start in range(0, query_ref.shape[0], rows):
        own = slice(start, start + rows)
        gain = gain_ref[own].astype(f32).reshape(1, rows)
        gain = jnp.where(row == column, gain, 0.0).astype(bf16)
        pieces = [query_ref[own, :PIECE], query_ref[own, PIECE:], keyval_ref[own, :]]
        for piece, out_ref in zip(pieces, out_refs):
            out_ref[own, :] = jnp.dot(gain, piece, preferred_element_type=f32).astype(bf16)


def fold(gain, query_weight, keyval_weight):
    pieces = WIDE // PIECE
    return pl.pallas_call(
        fold_kernel,
        out_shape=[jax.ShapeDtypeStruct((gain.shape[0], PIECE), bf16)] * pieces,
        in_specs=[VMEM] * 3,
        out_specs=[VMEM] * pieces,
        name="fold_gain",
    )(gain, query_weight, keyval_weight)


def inverse_kernel(rows_ref, inverse_ref, products):
    step = pl.program_id(0)
    rows = rows_ref[...]
    part = lax.dot_general(rows, rows, (((1,), (1,)), ((), ())), preferred_element_type=f32)

    @pl.when(step == 0)
    def _():
        products[...] = part

    @pl.when(step > 0)
    def _():
        products[...] += part

    @pl.when(step == pl.num_programs(0) - 1)
    def _():
        depth = pl.num_programs(0) * rows_ref.shape[1]
        row = lax.broadcasted_iota(jnp.int32, products.shape, 0)
        column = lax.broadcasted_iota(jnp.int32, products.shape, 1)
        squares = jnp.sum(jnp.where(row == column, products[...], 0.0), axis=1, keepdims=True)
        inverse_ref[...] = jnp.broadcast_to(lax.rsqrt(squares / depth + norm_eps), inverse_ref.shape)


def inverses(rows):
    tokens, depth = rows.shape
    steps = 4
    return pl.pallas_call(
        inverse_kernel,
        out_shape=jax.ShapeDtypeStruct((tokens, HD), f32),
        grid=(steps,),
        in_specs=[pl.BlockSpec((tokens, depth // steps), lambda i: (0, i))],
        out_specs=pl.BlockSpec((tokens, HD), lambda i: (0, 0)),
        scratch_shapes=[pltpu.VMEM((tokens, tokens), f32)],
        compiler_params=pltpu.CompilerParams(vmem_limit_bytes=60 << 20),
        cost_estimate=pl.CostEstimate(
            flops=2 * tokens * tokens * depth, bytes_accessed=2 * tokens * depth, transcendentals=0
        ),
        name="inverse",
    )(rows)


def partial_kernel(distances, sides, carried, *refs):
    pieces = WIDE // PIECE
    count = len(distances)
    weights, refs = refs[: count * pieces], refs[count * pieces :]
    rows, refs = refs[:sides], refs[sides:]
    before, refs = refs[: sides * carried], refs[sides * carried :]
    out_refs, (columns, arrived) = refs[:sides], refs[sides:]
    depth = columns.shape[2]
    index = lax.axis_index("fsdp")
    place, core = lax.div(index, 2), lax.rem(index, 2)
    ring = lax.axis_size("fsdp") // 2
    copies = []
    for side in range(sides):
        for i, distance in enumerate(distances):
            origin = lax.rem(place + ring + (2 * core - 1) * distance, ring)
            start = pl.multiple_of((2 * origin + core) * depth, depth)
            at = side * count + i
            copies.append(
                pltpu.make_async_copy(
                    rows[side].at[:, pl.ds(start, depth)], columns.at[at], arrived.at[at]
                )
            )
            copies[-1].start()
    for side in range(sides):
        for copy in copies[side * count : (side + 1) * count]:
            copy.wait()
        for piece in range(pieces):
            own = slice(piece * PIECE, (piece + 1) * PIECE)
            total = before[side][:, own] if carried else None
            for i in range(count):
                part = jnp.dot(
                    columns[side * count + i],
                    weights[i * pieces + piece][...],
                    preferred_element_type=f32,
                )
                total = part if total is None else total + part
            out_refs[side][:, own] = total


def partial(blocks, rows, before, vmem):
    count, sides = len(blocks), len(rows)
    weights = [w for _, pieces in blocks for w in pieces]
    tokens, depth = rows[0].shape[0], weights[0].shape[0]
    carried = before is not None
    shape = jax.ShapeDtypeStruct((tokens, WIDE), f32)
    return pl.pallas_call(
        functools.partial(partial_kernel, [d for d, _ in blocks], sides, carried),
        out_shape=[shape] * sides,
        in_specs=[VMEM] * len(weights)
        + [pl.BlockSpec(memory_space=pltpu.HBM)] * sides
        + [VMEM] * (sides * carried),
        out_specs=[VMEM] * sides,
        scratch_shapes=[
            pltpu.VMEM((sides * count, tokens, depth), bf16),
            pltpu.SemaphoreType.DMA((sides * count,)),
        ],
        compiler_params=pltpu.CompilerParams(vmem_limit_bytes=vmem << 20),
        cost_estimate=pl.CostEstimate(
            flops=2 * tokens * depth * WIDE * count * sides,
            bytes_accessed=2 * depth * (sides * tokens + WIDE) * count + 8 * tokens * WIDE * sides,
            transcendentals=0,
        ),
        name="partial_sums",
    )(*weights, *rows, *(before or []))


def attend_kernel(
    lengths_ref, learner_ref, offset_ref, mine_ref, other_ref, inverse_ref, cosine_ref, sine_ref, out_ref, mixed
):
    tokens = out_ref.shape[0]
    inverse = inverse_ref[...]
    cosine, sine = cosine_ref[...] * inverse, sine_ref[...] * inverse

    def product(head):
        own = slice(head * HD, (head + 1) * HD)
        return mine_ref[:, own] + other_ref[:, own]

    def rotated(head):
        values = product(head)
        return (values * cosine + pltpu.roll(values, HD // 2, 1) * sine).astype(bf16)

    heads = [rotated(h) for h in range(QH)]
    key_part = rotated(QH)
    value_part = (product(QH + 1) * inverse).astype(bf16)
    asks = lax.broadcasted_iota(jnp.int32, (PAIR, PAIR), 0)
    keys = lax.broadcasted_iota(jnp.int32, (PAIR, PAIR), 1)
    for pair in range(tokens // PAIR):
        own = slice(pair * PAIR, (pair + 1) * PAIR)
        lead = lengths_ref[2 * pair]
        allowed = (keys <= asks) & ((asks < lead) | (keys >= lead))
        barred = jnp.concatenate([jnp.where(allowed, 0.0, -1e30)] * QH, axis=0)
        query = jnp.concatenate([h[own] for h in heads], axis=0)
        scores = lax.dot_general(
            query, key_part[own], (((1,), (1,)), ((), ())), preferred_element_type=f32
        ) * (HD**-0.5)
        scores += barred
        weights = jnp.exp(scores - jnp.max(scores, axis=1, keepdims=True))
        share = 1.0 / jnp.sum(weights, axis=1, keepdims=True)
        probability = (weights * share).astype(bf16)
        result = jnp.dot(probability, value_part[own], preferred_element_type=f32).astype(bf16)
        for h in range(QH):
            mixed[own, h * HD : (h + 1) * HD] = result[h * PAIR : (h + 1) * PAIR]
    row = lax.broadcasted_iota(jnp.int32, (tokens, tokens), 0)
    token = lax.broadcasted_iota(jnp.int32, (tokens, tokens), 1)
    source = ((row >> 2) & 1) * PAIR + (row >> 3) * 4 + (row & 3)
    order = jnp.where(token == source, 1.0, 0.0).astype(bf16)
    out_ref[:, : QH * HD] = jnp.dot(order, mixed[...], preferred_element_type=f32).astype(bf16)
    lane = lax.broadcasted_iota(jnp.int32, (tokens, TABLE), 1)
    table = jnp.zeros((tokens, TABLE), jnp.int32)
    for i, ref in enumerate((lengths_ref, learner_ref, offset_ref)):
        for j in range(4):
            table = jnp.where(lane == 4 * i + j, ref[j], table)
    out_ref[:, QH * HD :] = table.astype(f32).astype(bf16)


def attend(lengths, learner, slot_offset, mine, other, inverse, cosine, sine):
    tokens = mine.shape[0]
    return pl.pallas_call(
        attend_kernel,
        out_shape=jax.ShapeDtypeStruct((tokens, QH * HD + TABLE), bf16),
        in_specs=[SMEM] * 3 + [VMEM] * 5,
        out_specs=VMEM,
        scratch_shapes=[pltpu.VMEM((tokens, QH * HD), bf16)],
        compiler_params=pltpu.CompilerParams(vmem_limit_bytes=16 << 20),
        name="attend",
    )(lengths, learner, slot_offset, mine, other, inverse, cosine, sine)


def rotary(lengths, tokens):
    slot = jnp.arange(tokens, dtype=jnp.int32)
    place = slot % PAIR
    lead = sum(jnp.where(slot // PAIR == k, lengths[2 * k], 0) for k in range(tokens // PAIR))
    position = jnp.where(place < lead, place, place - lead)
    lane = jnp.arange(HD, dtype=jnp.int32)
    frequency = rope_base ** (-(lane % (HD // 2)).astype(f32) * 2.0 / HD)
    angles = position.astype(f32)[:, None] * frequency[None, :]
    sign = jnp.where(lane < HD // 2, -1.0, 1.0)
    return jnp.cos(angles), jnp.sin(angles) * sign


def ranks(spread_ref):
    rows = spread_ref.shape[0]
    place = lax.broadcasted_iota(jnp.int32, (rows, 1), 0)
    table = spread_ref[:, QH * HD :].astype(f32)
    target = jnp.where((place >> 2) & 1 == 1, table[:, 6:7], table[:, 4:5])
    key = target * rows + (place >> 2).astype(f32)
    down = lax.broadcasted_iota(jnp.int32, (rows, rows), 0)
    along = lax.broadcasted_iota(jnp.int32, (rows, rows), 1)
    key_along = jnp.sum(jnp.where(down == along, key, 0.0), axis=0, keepdims=True)
    ahead_along = jnp.sum(jnp.where(key < key_along, 1.0, 0.0), axis=0, keepdims=True)
    return table, place, key, key_along, ahead_along.astype(jnp.int32), down


def arrange_kernel(spread_ref, out_ref):
    *_, ahead_along, down = ranks(spread_ref)
    row = lax.broadcasted_iota(jnp.int32, ahead_along.shape, 1)
    order = jnp.where(down == ahead_along + (row & 3), 1.0, 0.0).astype(bf16)
    out_ref[...] = jnp.dot(order, spread_ref[:, : QH * HD], preferred_element_type=f32).astype(bf16)


def slots_kernel(me_ref, spread_ref, out_ref):
    table, place, key, key_along, _, down = ranks(spread_ref)
    ahead = jnp.sum(jnp.where(key_along < key, 1.0, 0.0), axis=1, keepdims=True).astype(jnp.int32)
    second = (place >> 2) & 1 == 1
    row = lax.broadcasted_iota(jnp.int32, key_along.shape, 1)
    token = (row >> 3) * 4 + (row & 3)

    def slots(k):
        mine = (ahead == 4 * (2 * me_ref[0] + k)) & (place & 3 == 0)

        def own(even, odd):
            values = jnp.where(second, table[:, odd : odd + 1], table[:, even : even + 1])
            return jnp.sum(jnp.where(mine, values, 0.0), axis=0, keepdims=True).astype(jnp.int32)

        lead = own(0, 2)
        return jnp.where(token < lead, own(8, 10) + token, own(9, 11) + token - lead)

    slot = jnp.where((row >> 2) & 1 == 0, slots(0), slots(1))
    out_ref[...] = jnp.where(down == slot, 1.0, 0.0).astype(bf16)


def arrange(spread):
    return pl.pallas_call(
        arrange_kernel,
        out_shape=jax.ShapeDtypeStruct((spread.shape[0], QH * HD), bf16),
        in_specs=[VMEM],
        out_specs=VMEM,
        name="arrange",
    )(spread)


def slots(spread):
    return pl.pallas_call(
        slots_kernel,
        out_shape=jax.ShapeDtypeStruct((spread.shape[0],) * 2, bf16),
        in_specs=[SMEM, VMEM],
        out_specs=VMEM,
        name="slots",
    )(lax.axis_index("dp").reshape(1), spread)


def exchange(rows):
    blocks = rows.reshape(lax.axis_size("dp"), -1, rows.shape[1])
    return lax.all_to_all(blocks, "dp", split_axis=0, concat_axis=0, tiled=True).reshape(rows.shape)


def shards(hidden, lengths, learner, slot_offset, norm_gain, query_weight, keyval_weight):
    tokens = hidden.shape[0]
    size = lax.axis_size("fsdp")
    ring = size // 2
    onward = [(i, (i + 2 - 4 * (i % 2)) % size) for i in range(size)]
    swap = [(i, i ^ 1) for i in range(size)]

    def send(values, pairs):
        return lax.ppermute(values, "fsdp", pairs)

    def after(value, *others):
        return lax.optimization_barrier((value, *others))[0]

    moving = fold(norm_gain, query_weight, keyval_weight)
    blocks = [(0, list(moving))]
    sums = None
    got = send(hidden, swap)
    for step in range(1, ring):
        moving = [send(w, onward) for w in moving]
        if step == 3:
            inverse = inverses(after(hidden, moving[2]))
            cosine, sine = rotary(after(lengths, moving[2]), tokens)
        if step in (3, 5, ring - 1):
            sums = partial(blocks, (hidden, got), sums, 60)
            blocks = []
            moving[0] = after(moving[0], *sums)
        if step == 4:
            moving[0] = after(moving[0], inverse, cosine, sine)
        blocks += [(step, list(moving))]
    [other] = partial(blocks, (got,), sums[1:], 28)
    other = send(other, swap)
    [mine] = partial(blocks, (hidden,), sums[:1], 28)
    mixed = attend(lengths, learner, slot_offset, mine, other, inverse, cosine, sine)
    spread = exchange(mixed)
    landed = exchange(arrange(spread))
    return jnp.dot(slots(spread), landed, preferred_element_type=f32).astype(bf16)


def solution(mesh):
    placed = (
        P(("dp", "fsdp"), None),
        P(("dp", "fsdp")),
        P(("dp", "fsdp")),
        P(("dp", "fsdp")),
        P("fsdp"),
        P("fsdp", None),
        P("fsdp", None),
    )
    return jax.shard_map(
        shards, mesh=mesh, in_specs=placed, out_specs=P(("dp", "fsdp"), None), check_vma=False
    )
```

```python
import functools

import jax
import jax.numpy as jnp
from jax import lax
from jax.experimental import pallas as pl
from jax.experimental.pallas import tpu as pltpu
from jax.sharding import PartitionSpec as P

HD = 128
QH = 4
WIDE = (QH + 2) * HD
PAIR = 128
TABLE = 128

rope_base = 500000.0
norm_eps = 1e-05

f32 = jnp.float32
bf16 = jnp.bfloat16


VMEM = pl.BlockSpec(memory_space=pltpu.VMEM)
SMEM = pl.BlockSpec(memory_space=pltpu.SMEM)


def fold_kernel(gain_ref, query_ref, keyval_ref, *out_refs):
    rows = out_refs[0].shape[0]
    row = lax.broadcasted_iota(jnp.int32, (rows, rows), 0)
    column = lax.broadcasted_iota(jnp.int32, (rows, rows), 1)
    for i, out_ref in enumerate(out_refs):
        own = slice(i * rows, (i + 1) * rows)
        gain = gain_ref[own].astype(f32).reshape(1, rows)
        gain = jnp.where(row == column, gain, 0.0).astype(bf16)
        query = jnp.dot(gain, query_ref[own, :], preferred_element_type=f32)
        keyval = jnp.dot(gain, keyval_ref[own, :], preferred_element_type=f32)
        out_ref[:, : QH * HD] = query.astype(bf16)
        out_ref[:, QH * HD :] = keyval.astype(bf16)


def fold(gain, query_weight, keyval_weight):
    half = jax.ShapeDtypeStruct((gain.shape[0] // 2, WIDE), bf16)
    return pl.pallas_call(
        fold_kernel,
        out_shape=[half] * 2,
        in_specs=[VMEM] * 3,
        out_specs=[VMEM] * 2,
        name="fold_gain",
    )(gain, query_weight, keyval_weight)


def inverse_kernel(*refs):
    *rows_refs, inverse_ref, products = refs
    step = pl.program_id(0)
    part = sum(
        lax.dot_general(r[...], r[...], (((1,), (1,)), ((), ())), preferred_element_type=f32)
        for r in rows_refs
    )

    @pl.when(step == 0)
    def _():
        products[...] = part

    @pl.when(step > 0)
    def _():
        products[...] += part

    @pl.when(step == pl.num_programs(0) - 1)
    def _():
        depth = pl.num_programs(0) * sum(r.shape[1] for r in rows_refs)
        row = lax.broadcasted_iota(jnp.int32, products.shape, 0)
        column = lax.broadcasted_iota(jnp.int32, products.shape, 1)
        squares = jnp.sum(jnp.where(row == column, products[...], 0.0), axis=1, keepdims=True)
        inverse_ref[...] = jnp.broadcast_to(lax.rsqrt(squares / depth + norm_eps), inverse_ref.shape)


def inverses(rows):
    tokens, depth = rows.shape
    steps, streams = 4, 4
    block = depth // (steps * streams)

    def part(stream):
        return pl.BlockSpec((tokens, block), lambda i: (0, stream * steps + i))

    return pl.pallas_call(
        inverse_kernel,
        out_shape=jax.ShapeDtypeStruct((tokens, HD), f32),
        grid=(steps,),
        in_specs=[part(s) for s in range(streams)],
        out_specs=pl.BlockSpec((tokens, HD), lambda i: (0, 0)),
        scratch_shapes=[pltpu.VMEM((tokens, tokens), f32)],
        compiler_params=pltpu.CompilerParams(vmem_limit_bytes=60 << 20),
        cost_estimate=pl.CostEstimate(
            flops=2 * tokens * tokens * depth, bytes_accessed=2 * tokens * depth, transcendentals=0
        ),
        name="inverse",
    )(*[rows] * streams)


def partial_kernel(distances, sides, carried, *refs):
    count = len(distances)
    halves, refs = refs[: 2 * count], refs[2 * count :]
    rows, refs = refs[:sides], refs[sides:]
    before, refs = refs[: sides * carried], refs[sides * carried :]
    out_refs, (columns, weights, arrived) = refs[:sides], refs[sides:]
    depth = columns.shape[2]
    index = lax.axis_index("fsdp")
    place, core = lax.div(index, 2), lax.rem(index, 2)
    ring = lax.axis_size("fsdp") // 2
    copies = []

    def copy(source, target):
        copies.append(pltpu.make_async_copy(source, target, arrived.at[len(copies)]))
        copies[-1].start()

    for i, distance in enumerate(distances):
        origin = lax.rem(place + (ring + distance), ring)
        start = pl.multiple_of((2 * origin + core) * depth, depth)
        for side in range(sides):
            copy(rows[side].at[:, pl.ds(start, depth)], columns.at[side * count + i])
        for h in range(2):
            rest = pl.ds(h * (depth // 2), depth // 2)
            copy(halves[2 * i + h], weights.at[i, rest, :])
    for i in range(count):
        for c in copies[i * (sides + 2) : (i + 1) * (sides + 2)]:
            c.wait()
        for side in range(sides):
            part = jnp.dot(columns[side * count + i], weights[i], preferred_element_type=f32)
            if i:
                out_refs[side][...] += part
            else:
                out_refs[side][...] = before[side][...] + part if carried else part


def partial(blocks, rows, before, vmem):
    count, sides = len(blocks), len(rows)
    halves = [w for _, pair in blocks for w in pair]
    tokens, depth = rows[0].shape[0], 2 * halves[0].shape[0]
    carried = before is not None
    shape = jax.ShapeDtypeStruct((tokens, WIDE), f32)
    return pl.pallas_call(
        functools.partial(partial_kernel, [d for d, _ in blocks], sides, carried),
        out_shape=[shape] * sides,
        in_specs=[pl.BlockSpec(memory_space=pl.ANY)] * (len(halves) + sides)
        + [VMEM] * (sides * carried),
        out_specs=[VMEM] * sides,
        scratch_shapes=[
            pltpu.VMEM((sides * count, tokens, depth), bf16),
            pltpu.VMEM((count, depth, WIDE), bf16),
            pltpu.SemaphoreType.DMA((count * (sides + 2),)),
        ],
        compiler_params=pltpu.CompilerParams(vmem_limit_bytes=vmem << 20),
        cost_estimate=pl.CostEstimate(
            flops=2 * tokens * depth * WIDE * count * sides,
            bytes_accessed=2 * depth * (sides * tokens + WIDE) * count + 8 * tokens * WIDE * sides,
            transcendentals=0,
        ),
        name="partial_sums",
    )(*halves, *rows, *(before or []))


def attend_kernel(
    lengths_ref, learner_ref, offset_ref, mine_ref, other_ref, inverse_ref, cosine_ref, sine_ref, out_ref, mixed
):
    tokens = out_ref.shape[0]
    inverse = inverse_ref[...]
    cosine, sine = cosine_ref[...] * inverse, sine_ref[...] * inverse

    def product(head):
        own = slice(head * HD, (head + 1) * HD)
        return mine_ref[:, own] + other_ref[:, own]

    def rotated(head):
        values = product(head)
        return (values * cosine + pltpu.roll(values, HD // 2, 1) * sine).astype(bf16)

    heads = [rotated(h) for h in range(QH)]
    key_part = rotated(QH)
    value_part = (product(QH + 1) * inverse).astype(bf16)
    asks = lax.broadcasted_iota(jnp.int32, (PAIR, PAIR), 0)
    keys = lax.broadcasted_iota(jnp.int32, (PAIR, PAIR), 1)
    for pair in range(tokens // PAIR):
        own = slice(pair * PAIR, (pair + 1) * PAIR)
        lead = lengths_ref[2 * pair]
        allowed = (keys <= asks) & ((asks < lead) | (keys >= lead))
        barred = jnp.concatenate([jnp.where(allowed, 0.0, -1e30)] * QH, axis=0)
        query = jnp.concatenate([h[own] for h in heads], axis=0)
        scores = lax.dot_general(
            query, key_part[own], (((1,), (1,)), ((), ())), preferred_element_type=f32
        ) * (HD**-0.5)
        scores += barred
        weights = jnp.exp(scores - jnp.max(scores, axis=1, keepdims=True))
        share = 1.0 / jnp.sum(weights, axis=1, keepdims=True)
        probability = (weights * share).astype(bf16)
        result = jnp.dot(probability, value_part[own], preferred_element_type=f32).astype(bf16)
        for h in range(QH):
            mixed[own, h * HD : (h + 1) * HD] = result[h * PAIR : (h + 1) * PAIR]
    row = lax.broadcasted_iota(jnp.int32, (tokens, tokens), 0)
    token = lax.broadcasted_iota(jnp.int32, (tokens, tokens), 1)
    source = ((row >> 2) & 1) * PAIR + (row >> 3) * 4 + (row & 3)
    order = jnp.where(token == source, 1.0, 0.0).astype(bf16)
    out_ref[:, : QH * HD] = jnp.dot(order, mixed[...], preferred_element_type=f32).astype(bf16)
    lane = lax.broadcasted_iota(jnp.int32, (tokens, TABLE), 1)
    table = jnp.zeros((tokens, TABLE), jnp.int32)
    for i, ref in enumerate((lengths_ref, learner_ref, offset_ref)):
        for j in range(4):
            table = jnp.where(lane == 4 * i + j, ref[j], table)
    out_ref[:, QH * HD :] = table.astype(f32).astype(bf16)


def attend(lengths, learner, slot_offset, mine, other, inverse, cosine, sine):
    tokens = mine.shape[0]
    return pl.pallas_call(
        attend_kernel,
        out_shape=jax.ShapeDtypeStruct((tokens, QH * HD + TABLE), bf16),
        in_specs=[SMEM] * 3 + [VMEM] * 5,
        out_specs=VMEM,
        scratch_shapes=[pltpu.VMEM((tokens, QH * HD), bf16)],
        compiler_params=pltpu.CompilerParams(vmem_limit_bytes=16 << 20),
        name="attend",
    )(lengths, learner, slot_offset, mine, other, inverse, cosine, sine)


def rotary(lengths, tokens):
    slot = jnp.arange(tokens, dtype=jnp.int32)
    place = slot % PAIR
    lead = sum(jnp.where(slot // PAIR == k, lengths[2 * k], 0) for k in range(tokens // PAIR))
    position = jnp.where(place < lead, place, place - lead)
    lane = jnp.arange(HD, dtype=jnp.int32)
    frequency = rope_base ** (-(lane % (HD // 2)).astype(f32) * 2.0 / HD)
    angles = position.astype(f32)[:, None] * frequency[None, :]
    sign = jnp.where(lane < HD // 2, -1.0, 1.0)
    return jnp.cos(angles), jnp.sin(angles) * sign


def ranks(spread_ref):
    rows = spread_ref.shape[0]
    place = lax.broadcasted_iota(jnp.int32, (rows, 1), 0)
    table = spread_ref[:, QH * HD :].astype(f32)
    target = jnp.where((place >> 2) & 1 == 1, table[:, 6:7], table[:, 4:5])
    key = target * rows + (place >> 2).astype(f32)
    down = lax.broadcasted_iota(jnp.int32, (rows, rows), 0)
    along = lax.broadcasted_iota(jnp.int32, (rows, rows), 1)
    key_along = jnp.sum(jnp.where(down == along, key, 0.0), axis=0, keepdims=True)
    ahead_along = jnp.sum(jnp.where(key < key_along, 1.0, 0.0), axis=0, keepdims=True)
    return table, place, key, key_along, ahead_along.astype(jnp.int32), down


def arrange_kernel(spread_ref, out_ref):
    *_, ahead_along, down = ranks(spread_ref)
    row = lax.broadcasted_iota(jnp.int32, ahead_along.shape, 1)
    order = jnp.where(down == ahead_along + (row & 3), 1.0, 0.0).astype(bf16)
    out_ref[...] = jnp.dot(order, spread_ref[:, : QH * HD], preferred_element_type=f32).astype(bf16)


def slots_kernel(me_ref, spread_ref, out_ref):
    table, place, key, key_along, _, down = ranks(spread_ref)
    ahead = jnp.sum(jnp.where(key_along < key, 1.0, 0.0), axis=1, keepdims=True).astype(jnp.int32)
    second = (place >> 2) & 1 == 1
    row = lax.broadcasted_iota(jnp.int32, key_along.shape, 1)
    token = (row >> 3) * 4 + (row & 3)

    def slots(k):
        mine = (ahead == 4 * (2 * me_ref[0] + k)) & (place & 3 == 0)

        def own(even, odd):
            values = jnp.where(second, table[:, odd : odd + 1], table[:, even : even + 1])
            return jnp.sum(jnp.where(mine, values, 0.0), axis=0, keepdims=True).astype(jnp.int32)

        lead = own(0, 2)
        return jnp.where(token < lead, own(8, 10) + token, own(9, 11) + token - lead)

    slot = jnp.where((row >> 2) & 1 == 0, slots(0), slots(1))
    out_ref[...] = jnp.where(down == slot, 1.0, 0.0).astype(bf16)


def arrange(spread):
    return pl.pallas_call(
        arrange_kernel,
        out_shape=jax.ShapeDtypeStruct((spread.shape[0], QH * HD), bf16),
        in_specs=[VMEM],
        out_specs=VMEM,
        compiler_params=pltpu.CompilerParams(vmem_limit_bytes=16 << 20),
        name="arrange",
    )(spread)


def slots(spread):
    return pl.pallas_call(
        slots_kernel,
        out_shape=jax.ShapeDtypeStruct((spread.shape[0],) * 2, bf16),
        in_specs=[SMEM, VMEM],
        out_specs=VMEM,
        compiler_params=pltpu.CompilerParams(vmem_limit_bytes=16 << 20),
        name="slots",
    )(lax.axis_index("dp").reshape(1), spread)


def exchange(rows):
    blocks = rows.reshape(lax.axis_size("dp"), -1, rows.shape[1])
    return lax.all_to_all(blocks, "dp", split_axis=0, concat_axis=0, tiled=True).reshape(rows.shape)


def shards(hidden, lengths, learner, slot_offset, norm_gain, query_weight, keyval_weight):
    tokens = hidden.shape[0]
    size = lax.axis_size("fsdp")
    ring = size // 2
    up = [(i, (i + 2) % size) for i in range(size)]
    down = [(i, (i - 2) % size) for i in range(size)]
    swap = [(i, i ^ 1) for i in range(size)]

    def send(values, pairs):
        return lax.ppermute(values, "fsdp", pairs)

    def after(value, *others):
        return lax.optimization_barrier((value, *others))[0]

    held = fold(norm_gain, query_weight, keyval_weight)
    got = send(hidden, swap)
    above, below = list(held), list(held)
    blocks = [(0, held)]
    for step in range(1, ring // 2):
        above = [send(w, up) for w in above]
        below = [send(w, down) for w in below]
        if step == 1:
            inverse = inverses(after(hidden, above[1]))
            cosine, sine = rotary(after(lengths, above[1]), tokens)
        if step == 2:
            above[0] = after(above[0], inverse, cosine, sine)
        blocks += [(-step, list(above)), (step, list(below))]
    far = [send(above[0], up), send(below[1], down)]
    sums = partial(blocks, (hidden, got), None, 60)
    far[1] = after(far[1], *sums)
    [other] = partial([(ring // 2, far)], (got,), sums[1:], 28)
    other = send(other, swap)
    [mine] = partial([(ring // 2, far)], (hidden,), sums[:1], 28)
    mixed = attend(lengths, learner, slot_offset, mine, other, inverse, cosine, sine)
    spread = exchange(mixed)
    landed = exchange(arrange(spread))
    return jnp.dot(slots(spread), landed, preferred_element_type=f32).astype(bf16)


def solution(mesh):
    placed = (
        P(("dp", "fsdp"), None),
        P(("dp", "fsdp")),
        P(("dp", "fsdp")),
        P(("dp", "fsdp")),
        P("fsdp"),
        P("fsdp", None),
        P("fsdp", None),
    )
    return jax.shard_map(
        shards, mesh=mesh, in_specs=placed, out_specs=P(("dp", "fsdp"), None), check_vma=False
    )
```

```python
import functools

import jax
import jax.numpy as jnp
import numpy as np
from jax import lax
from jax.experimental import pallas as pl
from jax.experimental.pallas import tpu as pltpu
from jax.sharding import PartitionSpec as P

HD = 128
QH = 4
WIDE = (QH + 2) * HD
PAIR = 128
TABLE = 128

rope_base = 500000.0
norm_eps = 1e-05

f32 = jnp.float32
bf16 = jnp.bfloat16


VMEM = pl.BlockSpec(memory_space=pltpu.VMEM)
SMEM = pl.BlockSpec(memory_space=pltpu.SMEM)


def fold_kernel(gain_ref, query_ref, keyval_ref, *out_refs):
    rows = out_refs[0].shape[0]
    row = lax.broadcasted_iota(jnp.int32, (rows, rows), 0)
    column = lax.broadcasted_iota(jnp.int32, (rows, rows), 1)
    for i, out_ref in enumerate(out_refs):
        own = slice(i * rows, (i + 1) * rows)
        gain = gain_ref[own].astype(f32).reshape(1, rows)
        gain = jnp.where(row == column, gain, 0.0).astype(bf16)
        query = jnp.dot(gain, query_ref[own, :], preferred_element_type=f32)
        keyval = jnp.dot(gain, keyval_ref[own, :], preferred_element_type=f32)
        out_ref[:, : QH * HD] = query.astype(bf16)
        out_ref[:, QH * HD :] = keyval.astype(bf16)


def fold(gain, query_weight, keyval_weight):
    half = jax.ShapeDtypeStruct((gain.shape[0] // 2, WIDE), bf16)
    return pl.pallas_call(
        fold_kernel,
        out_shape=[half] * 2,
        in_specs=[VMEM] * 3,
        out_specs=[VMEM] * 2,
        name="fold_gain",
    )(gain, query_weight, keyval_weight)


def inverse_kernel(*refs):
    *rows_refs, inverse_ref, squares = refs
    step = pl.program_id(0)

    @pl.when(step == 0)
    def _():
        squares[...] = jnp.zeros_like(squares)

    total = squares[...]
    for ref in rows_refs:
        for i in range(ref.shape[1] // HD):
            total += jnp.square(ref[:, i * HD : (i + 1) * HD].astype(f32))
    squares[...] = total

    @pl.when(step == pl.num_programs(0) - 1)
    def _():
        depth = pl.num_programs(0) * sum(r.shape[1] for r in rows_refs)
        mean = jnp.sum(squares[...], axis=1, keepdims=True) / depth
        inverse_ref[...] = jnp.broadcast_to(lax.rsqrt(mean + norm_eps), inverse_ref.shape)


def inverses(rows):
    tokens, depth = rows.shape
    steps, streams = 4, 4
    block = depth // (steps * streams)

    def part(stream):
        return pl.BlockSpec((tokens, block), lambda i: (0, stream * steps + i))

    return pl.pallas_call(
        inverse_kernel,
        out_shape=jax.ShapeDtypeStruct((tokens, HD), f32),
        grid=(steps,),
        in_specs=[part(s) for s in range(streams)],
        out_specs=pl.BlockSpec((tokens, HD), lambda i: (0, 0)),
        scratch_shapes=[pltpu.VMEM((tokens, HD), f32)],
        compiler_params=pltpu.CompilerParams(vmem_limit_bytes=60 << 20),
        cost_estimate=pl.CostEstimate(
            flops=2 * tokens * depth, bytes_accessed=2 * tokens * depth, transcendentals=0
        ),
        name="inverse",
    )(*[rows] * streams)


def partial_kernel(distances, sides, carried, *refs):
    count = len(distances)
    halves, refs = refs[: 2 * count], refs[2 * count :]
    rows, refs = refs[:sides], refs[sides:]
    before, refs = refs[: sides * carried], refs[sides * carried :]
    out_refs, (columns, weights, arrived) = refs[:sides], refs[sides:]
    depth = columns.shape[2]
    index = lax.axis_index("fsdp")
    place, core = lax.div(index, 2), lax.rem(index, 2)
    ring = lax.axis_size("fsdp") // 2
    copies = []

    def copy(source, target):
        copies.append(pltpu.make_async_copy(source, target, arrived.at[len(copies)]))
        copies[-1].start()

    for source, out_ref in zip(before, out_refs):
        copy(source, out_ref)
    for i, distance in enumerate(distances):
        origin = lax.rem(place + (ring + distance), ring)
        start = pl.multiple_of((2 * origin + core) * depth, depth)
        for side in range(sides):
            copy(rows[side].at[:, pl.ds(start, depth)], columns.at[side * count + i])
        for h in range(2):
            rest = pl.ds(h * (depth // 2), depth // 2)
            copy(halves[2 * i + h], weights.at[i, rest, :])
    for i in range(count):
        known = len(before) + (i + 1) * (sides + 2)
        for c in copies[0 if i == 0 else known - sides - 2 : known]:
            c.wait()
        for side in range(sides):
            part = jnp.dot(columns[side * count + i], weights[i], preferred_element_type=f32)
            if i or carried:
                out_refs[side][...] += part
            else:
                out_refs[side][...] = part


def partial(blocks, rows, before, vmem):
    count, sides = len(blocks), len(rows)
    halves = [w for _, pair in blocks for w in pair]
    tokens, depth = rows[0].shape[0], 2 * halves[0].shape[0]
    carried = before is not None
    shape = jax.ShapeDtypeStruct((tokens, WIDE), f32)
    return pl.pallas_call(
        functools.partial(partial_kernel, [d for d, _ in blocks], sides, carried),
        out_shape=[shape] * sides,
        in_specs=[pl.BlockSpec(memory_space=pl.ANY)] * (len(halves) + sides + sides * carried),
        out_specs=[VMEM] * sides,
        scratch_shapes=[
            pltpu.VMEM((sides * count, tokens, depth), bf16),
            pltpu.VMEM((count, depth, WIDE), bf16),
            pltpu.SemaphoreType.DMA((count * (sides + 2) + sides * carried,)),
        ],
        compiler_params=pltpu.CompilerParams(vmem_limit_bytes=vmem << 20),
        cost_estimate=pl.CostEstimate(
            flops=2 * tokens * depth * WIDE * count * sides,
            bytes_accessed=2 * depth * (sides * tokens + WIDE) * count + 8 * tokens * WIDE * sides,
            transcendentals=0,
        ),
        name="partial_sums",
    )(*halves, *rows, *(before or []))


def attend_kernel(
    lengths_ref, learner_ref, offset_ref, mine_ref, other_ref, inverse_ref, cosine_ref, sine_ref, out_ref, mixed
):
    tokens = out_ref.shape[0]
    inverse = inverse_ref[...]

    def by_position(table_ref):
        table = table_ref[...]
        place = lax.broadcasted_iota(jnp.int32, table.shape, 0)
        leads = [lengths_ref[2 * k] for k in range(tokens // PAIR)]
        pairs = [jnp.where(place < n, table, pltpu.roll(table, n, 0)) for n in leads]
        return jnp.concatenate(pairs, axis=0) * inverse

    cosine, sine = by_position(cosine_ref), by_position(sine_ref)

    def product(head):
        own = slice(head * HD, (head + 1) * HD)
        return mine_ref[:, own] + other_ref[:, own]

    def rotated(head):
        values = product(head)
        return (values * cosine + pltpu.roll(values, HD // 2, 1) * sine).astype(bf16)

    heads = [rotated(h) for h in range(QH)]
    key_part = rotated(QH)
    value_part = (product(QH + 1) * inverse).astype(bf16)
    asks = lax.broadcasted_iota(jnp.int32, (PAIR, PAIR), 0)
    keys = lax.broadcasted_iota(jnp.int32, (PAIR, PAIR), 1)
    for pair in range(tokens // PAIR):
        own = slice(pair * PAIR, (pair + 1) * PAIR)
        lead = lengths_ref[2 * pair]
        allowed = (keys <= asks) & ((asks < lead) | (keys >= lead))
        barred = jnp.concatenate([jnp.where(allowed, 0.0, -1e30)] * QH, axis=0)
        query = jnp.concatenate([h[own] for h in heads], axis=0)
        scores = lax.dot_general(
            query, key_part[own], (((1,), (1,)), ((), ())), preferred_element_type=f32
        ) * (HD**-0.5)
        scores += barred
        weights = jnp.exp(scores - jnp.max(scores, axis=1, keepdims=True))
        share = 1.0 / jnp.sum(weights, axis=1, keepdims=True)
        probability = (weights * share).astype(bf16)
        result = jnp.dot(probability, value_part[own], preferred_element_type=f32).astype(bf16)
        for h in range(QH):
            mixed[own, h * HD : (h + 1) * HD] = result[h * PAIR : (h + 1) * PAIR]
    row = lax.broadcasted_iota(jnp.int32, (tokens, tokens), 0)
    token = lax.broadcasted_iota(jnp.int32, (tokens, tokens), 1)
    source = ((row >> 2) & 1) * PAIR + (row >> 3) * 4 + (row & 3)
    order = jnp.where(token == source, 1.0, 0.0).astype(bf16)
    out_ref[:, : QH * HD] = jnp.dot(order, mixed[...], preferred_element_type=f32).astype(bf16)
    lane = lax.broadcasted_iota(jnp.int32, (tokens, TABLE), 1)
    table = jnp.zeros((tokens, TABLE), jnp.int32)
    for i, ref in enumerate((lengths_ref, learner_ref, offset_ref)):
        for j in range(4):
            table = jnp.where(lane == 4 * i + j, ref[j], table)
    out_ref[:, QH * HD :] = table.astype(f32).astype(bf16)


def attend(lengths, learner, slot_offset, mine, other, inverse, cosine, sine):
    tokens = mine.shape[0]
    return pl.pallas_call(
        attend_kernel,
        out_shape=jax.ShapeDtypeStruct((tokens, QH * HD + TABLE), bf16),
        in_specs=[SMEM] * 3 + [VMEM] * 5,
        out_specs=VMEM,
        scratch_shapes=[pltpu.VMEM((tokens, QH * HD), bf16)],
        compiler_params=pltpu.CompilerParams(vmem_limit_bytes=16 << 20),
        name="attend",
    )(lengths, learner, slot_offset, mine, other, inverse, cosine, sine)


def rotary():
    lane = np.arange(HD)
    frequency = rope_base ** (-(lane % (HD // 2)) * 2.0 / HD)
    angles = np.arange(PAIR)[:, None] * frequency[None, :]
    sine = np.where(lane < HD // 2, -1.0, 1.0) * np.sin(angles)
    return np.cos(angles).astype(np.float32), sine.astype(np.float32)


def ranks(spread_ref):
    rows = spread_ref.shape[0]
    place = lax.broadcasted_iota(jnp.int32, (rows, 1), 0)
    table = spread_ref[:, QH * HD :].astype(f32)
    target = jnp.where((place >> 2) & 1 == 1, table[:, 6:7], table[:, 4:5])
    key = target * rows + (place >> 2).astype(f32)
    down = lax.broadcasted_iota(jnp.int32, (rows, rows), 0)
    along = lax.broadcasted_iota(jnp.int32, (rows, rows), 1)
    key_along = jnp.sum(jnp.where(down == along, key, 0.0), axis=0, keepdims=True)
    ahead_along = jnp.sum(jnp.where(key < key_along, 1.0, 0.0), axis=0, keepdims=True)
    return table, place, key, key_along, ahead_along.astype(jnp.int32), down


def arrange_kernel(spread_ref, out_ref):
    *_, ahead_along, down = ranks(spread_ref)
    row = lax.broadcasted_iota(jnp.int32, ahead_along.shape, 1)
    order = jnp.where(down == ahead_along + (row & 3), 1.0, 0.0).astype(bf16)
    out_ref[...] = jnp.dot(order, spread_ref[:, : QH * HD], preferred_element_type=f32).astype(bf16)


def slots_kernel(me_ref, spread_ref, out_ref):
    table, place, key, key_along, _, down = ranks(spread_ref)
    ahead = jnp.sum(jnp.where(key_along < key, 1.0, 0.0), axis=1, keepdims=True).astype(jnp.int32)
    second = (place >> 2) & 1 == 1
    row = lax.broadcasted_iota(jnp.int32, key_along.shape, 1)
    token = (row >> 3) * 4 + (row & 3)

    def slots(k):
        mine = (ahead == 4 * (2 * me_ref[0] + k)) & (place & 3 == 0)

        def own(even, odd):
            values = jnp.where(second, table[:, odd : odd + 1], table[:, even : even + 1])
            return jnp.sum(jnp.where(mine, values, 0.0), axis=0, keepdims=True).astype(jnp.int32)

        lead = own(0, 2)
        return jnp.where(token < lead, own(8, 10) + token, own(9, 11) + token - lead)

    slot = jnp.where((row >> 2) & 1 == 0, slots(0), slots(1))
    out_ref[...] = jnp.where(down == slot, 1.0, 0.0).astype(bf16)


def arrange(spread):
    return pl.pallas_call(
        arrange_kernel,
        out_shape=jax.ShapeDtypeStruct((spread.shape[0], QH * HD), bf16),
        in_specs=[VMEM],
        out_specs=VMEM,
        compiler_params=pltpu.CompilerParams(vmem_limit_bytes=16 << 20),
        name="arrange",
    )(spread)


def slots(spread):
    return pl.pallas_call(
        slots_kernel,
        out_shape=jax.ShapeDtypeStruct((spread.shape[0],) * 2, bf16),
        in_specs=[SMEM, VMEM],
        out_specs=VMEM,
        compiler_params=pltpu.CompilerParams(vmem_limit_bytes=16 << 20),
        name="slots",
    )(lax.axis_index("dp").reshape(1), spread)


def exchange(rows):
    blocks = rows.reshape(lax.axis_size("dp"), -1, rows.shape[1])
    return lax.all_to_all(blocks, "dp", split_axis=0, concat_axis=0, tiled=True).reshape(rows.shape)


def shards(hidden, lengths, learner, slot_offset, norm_gain, query_weight, keyval_weight):
    tokens = hidden.shape[0]
    size = lax.axis_size("fsdp")
    ring = size // 2
    up = [(i, (i + 2) % size) for i in range(size)]
    down = [(i, (i - 2) % size) for i in range(size)]
    swap = [(i, i ^ 1) for i in range(size)]

    def send(values, pairs):
        return lax.ppermute(values, "fsdp", pairs)

    def after(value, *others):
        return lax.optimization_barrier((value, *others))[0]

    held = fold(norm_gain, query_weight, keyval_weight)
    got = send(hidden, swap)
    inverse = inverses(after(hidden, held[0]))
    above, below = list(held), list(held)
    blocks = [(0, held)]
    for step in range(1, ring // 2):
        above = [send(w, up) for w in above]
        below = [send(w, down) for w in below]
        if step == 1:
            above[0] = after(above[0], inverse)
        blocks += [(-step, list(above)), (step, list(below))]
    far = [send(above[0], up), send(below[1], down)]
    sums = partial(blocks, (hidden, got), None, 28)
    far[1] = after(far[1], *sums)
    [other] = partial([(ring // 2, far)], (got,), sums[1:], 28)
    other = send(other, swap)
    [mine] = partial([(ring // 2, far)], (hidden,), sums[:1], 28)
    mixed = attend(lengths, learner, slot_offset, mine, other, inverse, *rotary())
    spread = exchange(mixed)
    landed = exchange(arrange(spread))
    return jnp.dot(slots(spread), landed, preferred_element_type=f32).astype(bf16)


def solution(mesh):
    placed = (
        P(("dp", "fsdp"), None),
        P(("dp", "fsdp")),
        P(("dp", "fsdp")),
        P(("dp", "fsdp")),
        P("fsdp"),
        P("fsdp", None),
        P("fsdp", None),
    )
    return jax.shard_map(
        shards, mesh=mesh, in_specs=placed, out_specs=P(("dp", "fsdp"), None), check_vma=False
    )
```

```python
import functools

import jax
import jax.numpy as jnp
import numpy as np
from jax import lax
from jax.experimental import pallas as pl
from jax.experimental.pallas import tpu as pltpu
from jax.sharding import PartitionSpec as P

HD = 128
QH = 4
WIDE = (QH + 2) * HD
PAIR = 128
TABLE = 128

rope_base = 500000.0
norm_eps = 1e-05

f32 = jnp.float32
bf16 = jnp.bfloat16


VMEM = pl.BlockSpec(memory_space=pltpu.VMEM)
SMEM = pl.BlockSpec(memory_space=pltpu.SMEM)


def fold_kernel(gain_ref, query_ref, keyval_ref, *out_refs):
    rows = out_refs[0].shape[0]
    row = lax.broadcasted_iota(jnp.int32, (rows, rows), 0)
    column = lax.broadcasted_iota(jnp.int32, (rows, rows), 1)
    for i, out_ref in enumerate(out_refs):
        own = slice(i * rows, (i + 1) * rows)
        gain = gain_ref[own].astype(f32).reshape(1, rows)
        gain = jnp.where(row == column, gain, 0.0).astype(bf16)
        query = jnp.dot(gain, query_ref[own, :], preferred_element_type=f32)
        keyval = jnp.dot(gain, keyval_ref[own, :], preferred_element_type=f32)
        out_ref[:, : QH * HD] = query.astype(bf16)
        out_ref[:, QH * HD :] = keyval.astype(bf16)


def fold(gain, query_weight, keyval_weight):
    half = jax.ShapeDtypeStruct((gain.shape[0] // 2, WIDE), bf16)
    return pl.pallas_call(
        fold_kernel,
        out_shape=[half] * 2,
        in_specs=[VMEM] * 3,
        out_specs=[VMEM] * 2,
        name="fold_gain",
    )(gain, query_weight, keyval_weight)


def inverse_kernel(rows_ref, inverse_ref):
    tokens, depth = rows_ref.shape
    chunk = 4 * HD

    def add(i, total):
        rows = rows_ref[:, pl.ds(pl.multiple_of(i * chunk, chunk), chunk)]
        for j in range(0, chunk, HD):
            total += jnp.square(rows[:, j : j + HD].astype(f32))
        return total

    total = lax.fori_loop(0, depth // chunk, add, jnp.zeros((tokens, HD), f32))
    mean = jnp.sum(total, axis=1, keepdims=True) / depth
    inverse_ref[...] = jnp.broadcast_to(lax.rsqrt(mean + norm_eps), inverse_ref.shape)


def inverses(rows):
    tokens, depth = rows.shape
    return pl.pallas_call(
        inverse_kernel,
        out_shape=jax.ShapeDtypeStruct((tokens, HD), f32),
        in_specs=[VMEM],
        out_specs=VMEM,
        compiler_params=pltpu.CompilerParams(vmem_limit_bytes=24 << 20),
        cost_estimate=pl.CostEstimate(
            flops=2 * tokens * depth, bytes_accessed=2 * tokens * depth, transcendentals=0
        ),
        name="inverse",
    )(rows)


def partial_kernel(distances, sides, carried, *refs):
    count = len(distances)
    halves, refs = refs[: 2 * count], refs[2 * count :]
    rows, refs = refs[:sides], refs[sides:]
    before, refs = refs[: sides * carried], refs[sides * carried :]
    out_refs, (columns, arrived) = refs[:sides], refs[sides:]
    half = halves[0].shape[0]
    index = lax.axis_index("fsdp")
    place, core = lax.div(index, 2), lax.rem(index, 2)
    ring = lax.axis_size("fsdp") // 2
    copies = []
    for side in range(sides):
        for i, distance in enumerate(distances):
            origin = lax.rem(place + (ring + distance), ring)
            start = pl.multiple_of((2 * origin + core) * (2 * half), 2 * half)
            at = side * count + i
            copies.append(
                pltpu.make_async_copy(
                    rows[side].at[:, pl.ds(start, 2 * half)], columns.at[at], arrived.at[at]
                )
            )
            copies[-1].start()
    for side in range(sides):
        total = before[side][...] if carried else None
        for i in range(count):
            at = side * count + i
            copies[at].wait()
            for h in range(2):
                part = jnp.dot(
                    columns[at, :, h * half : (h + 1) * half],
                    halves[2 * i + h][...],
                    preferred_element_type=f32,
                )
                total = part if total is None else total + part
        out_refs[side][...] = total


def partial(blocks, rows, before):
    count, sides = len(blocks), len(rows)
    halves = [w for _, pair in blocks for w in pair]
    tokens, depth = rows[0].shape[0], 2 * halves[0].shape[0]
    carried = before is not None
    operands = [*halves, *rows, *(before or [])]
    return pl.pallas_call(
        functools.partial(partial_kernel, [d for d, _ in blocks], sides, carried),
        out_shape=[jax.ShapeDtypeStruct((tokens, WIDE), f32)] * sides,
        in_specs=[VMEM] * len(halves)
        + [pl.BlockSpec(memory_space=pl.ANY)] * sides
        + [VMEM] * (sides * carried),
        out_specs=[VMEM] * sides,
        scratch_shapes=[
            pltpu.VMEM((sides * count, tokens, depth), bf16),
            pltpu.SemaphoreType.DMA((sides * count,)),
        ],
        compiler_params=pltpu.CompilerParams(vmem_limit_bytes=28 << 20),
        cost_estimate=pl.CostEstimate(
            flops=2 * tokens * depth * WIDE * count * sides,
            bytes_accessed=2 * depth * (sides * tokens + WIDE) * count + 8 * tokens * WIDE * sides,
            transcendentals=0,
        ),
        name="partial_sums",
    )(*operands)


def attend_kernel(
    lengths_ref, learner_ref, offset_ref, mine_ref, other_ref, inverse_ref, cosine_ref, sine_ref, out_ref, mixed
):
    tokens = out_ref.shape[0]
    inverse = inverse_ref[...]

    def by_position(table_ref):
        table = table_ref[...]
        place = lax.broadcasted_iota(jnp.int32, table.shape, 0)
        leads = [lengths_ref[2 * k] for k in range(tokens // PAIR)]
        pairs = [jnp.where(place < n, table, pltpu.roll(table, n, 0)) for n in leads]
        return jnp.concatenate(pairs, axis=0) * inverse

    cosine, sine = by_position(cosine_ref), by_position(sine_ref)

    def product(head):
        own = slice(head * HD, (head + 1) * HD)
        return mine_ref[:, own] + other_ref[:, own]

    def rotated(head):
        values = product(head)
        return (values * cosine + pltpu.roll(values, HD // 2, 1) * sine).astype(bf16)

    heads = [rotated(h) for h in range(QH)]
    key_part = rotated(QH)
    value_part = (product(QH + 1) * inverse).astype(bf16)
    asks = lax.broadcasted_iota(jnp.int32, (PAIR, PAIR), 0)
    keys = lax.broadcasted_iota(jnp.int32, (PAIR, PAIR), 1)
    for pair in range(tokens // PAIR):
        own = slice(pair * PAIR, (pair + 1) * PAIR)
        lead = lengths_ref[2 * pair]
        allowed = (keys <= asks) & ((asks < lead) | (keys >= lead))
        barred = jnp.concatenate([jnp.where(allowed, 0.0, -1e30)] * QH, axis=0)
        query = jnp.concatenate([h[own] for h in heads], axis=0)
        scores = lax.dot_general(
            query, key_part[own], (((1,), (1,)), ((), ())), preferred_element_type=f32
        ) * (HD**-0.5)
        scores += barred
        weights = jnp.exp(scores - jnp.max(scores, axis=1, keepdims=True))
        share = 1.0 / jnp.sum(weights, axis=1, keepdims=True)
        probability = (weights * share).astype(bf16)
        result = jnp.dot(probability, value_part[own], preferred_element_type=f32).astype(bf16)
        for h in range(QH):
            mixed[own, h * HD : (h + 1) * HD] = result[h * PAIR : (h + 1) * PAIR]
    row = lax.broadcasted_iota(jnp.int32, (tokens, tokens), 0)
    token = lax.broadcasted_iota(jnp.int32, (tokens, tokens), 1)
    source = ((row >> 2) & 1) * PAIR + (row >> 3) * 4 + (row & 3)
    order = jnp.where(token == source, 1.0, 0.0).astype(bf16)
    out_ref[:, : QH * HD] = jnp.dot(order, mixed[...], preferred_element_type=f32).astype(bf16)
    lane = lax.broadcasted_iota(jnp.int32, (tokens, TABLE), 1)
    table = jnp.zeros((tokens, TABLE), jnp.int32)
    for i, ref in enumerate((lengths_ref, learner_ref, offset_ref)):
        for j in range(4):
            table = jnp.where(lane == 4 * i + j, ref[j], table)
    out_ref[:, QH * HD :] = table.astype(f32).astype(bf16)


def attend(lengths, learner, slot_offset, mine, other, inverse, cosine, sine):
    tokens = mine.shape[0]
    return pl.pallas_call(
        attend_kernel,
        out_shape=jax.ShapeDtypeStruct((tokens, QH * HD + TABLE), bf16),
        in_specs=[SMEM] * 3 + [VMEM] * 5,
        out_specs=VMEM,
        scratch_shapes=[pltpu.VMEM((tokens, QH * HD), bf16)],
        compiler_params=pltpu.CompilerParams(vmem_limit_bytes=16 << 20),
        name="attend",
    )(lengths, learner, slot_offset, mine, other, inverse, cosine, sine)


def rotary():
    lane = np.arange(HD)
    frequency = rope_base ** (-(lane % (HD // 2)) * 2.0 / HD)
    angles = np.arange(PAIR)[:, None] * frequency[None, :]
    sine = np.where(lane < HD // 2, -1.0, 1.0) * np.sin(angles)
    return np.cos(angles).astype(np.float32), sine.astype(np.float32)


def ranks(spread_ref):
    rows = spread_ref.shape[0]
    place = lax.broadcasted_iota(jnp.int32, (rows, 1), 0)
    table = spread_ref[:, QH * HD :].astype(f32)
    target = jnp.where((place >> 2) & 1 == 1, table[:, 6:7], table[:, 4:5])
    key = target * rows + (place >> 2).astype(f32)
    down = lax.broadcasted_iota(jnp.int32, (rows, rows), 0)
    along = lax.broadcasted_iota(jnp.int32, (rows, rows), 1)
    key_along = jnp.sum(jnp.where(down == along, key, 0.0), axis=0, keepdims=True)
    ahead_along = jnp.sum(jnp.where(key < key_along, 1.0, 0.0), axis=0, keepdims=True)
    return table, place, key, key_along, ahead_along.astype(jnp.int32), down


def arrange_kernel(spread_ref, out_ref):
    *_, ahead_along, down = ranks(spread_ref)
    row = lax.broadcasted_iota(jnp.int32, ahead_along.shape, 1)
    order = jnp.where(down == ahead_along + (row & 3), 1.0, 0.0).astype(bf16)
    out_ref[...] = jnp.dot(order, spread_ref[:, : QH * HD], preferred_element_type=f32).astype(bf16)


def slots_kernel(me_ref, spread_ref, out_ref):
    table, place, key, key_along, _, down = ranks(spread_ref)
    ahead = jnp.sum(jnp.where(key_along < key, 1.0, 0.0), axis=1, keepdims=True).astype(jnp.int32)
    second = (place >> 2) & 1 == 1
    row = lax.broadcasted_iota(jnp.int32, key_along.shape, 1)
    token = (row >> 3) * 4 + (row & 3)

    def slots(k):
        mine = (ahead == 4 * (2 * me_ref[0] + k)) & (place & 3 == 0)

        def own(even, odd):
            values = jnp.where(second, table[:, odd : odd + 1], table[:, even : even + 1])
            return jnp.sum(jnp.where(mine, values, 0.0), axis=0, keepdims=True).astype(jnp.int32)

        lead = own(0, 2)
        return jnp.where(token < lead, own(8, 10) + token, own(9, 11) + token - lead)

    slot = jnp.where((row >> 2) & 1 == 0, slots(0), slots(1))
    out_ref[...] = jnp.where(down == slot, 1.0, 0.0).astype(bf16)


def arrange(spread):
    return pl.pallas_call(
        arrange_kernel,
        out_shape=jax.ShapeDtypeStruct((spread.shape[0], QH * HD), bf16),
        in_specs=[VMEM],
        out_specs=VMEM,
        compiler_params=pltpu.CompilerParams(vmem_limit_bytes=16 << 20),
        name="arrange",
    )(spread)


def slots(spread):
    return pl.pallas_call(
        slots_kernel,
        out_shape=jax.ShapeDtypeStruct((spread.shape[0],) * 2, bf16),
        in_specs=[SMEM, VMEM],
        out_specs=VMEM,
        compiler_params=pltpu.CompilerParams(vmem_limit_bytes=16 << 20),
        name="slots",
    )(lax.axis_index("dp").reshape(1), spread)


def exchange(rows):
    blocks = rows.reshape(lax.axis_size("dp"), -1, rows.shape[1])
    return lax.all_to_all(blocks, "dp", split_axis=0, concat_axis=0, tiled=True).reshape(rows.shape)


def shards(hidden, lengths, learner, slot_offset, norm_gain, query_weight, keyval_weight):
    tokens = hidden.shape[0]
    size = lax.axis_size("fsdp")
    ring = size // 2
    up = [(i, (i + 2) % size) for i in range(size)]
    down = [(i, (i - 2) % size) for i in range(size)]
    swap = [(i, i ^ 1) for i in range(size)]

    def send(values, pairs):
        return lax.ppermute(values, "fsdp", pairs)

    def after(value, *others):
        return lax.optimization_barrier((value, *others))[0]

    held = fold(norm_gain, query_weight, keyval_weight)
    got = send(hidden, swap)
    above, below = list(held), list(held)
    blocks = [(0, held)]
    for step in range(1, ring // 2):
        above = [send(w, up) for w in above]
        below = [send(w, down) for w in below]
        blocks += [(-step, list(above)), (step, list(below))]
    far = [send(above[0], up), send(below[1], down)]
    both = (hidden, got)
    sums = partial(blocks[:-2], both, None)
    sums = partial([(d, (a, after(b, *sums))) for d, (a, b) in blocks[-2:]], both, sums)
    inverse = inverses(after(hidden, sums[0]))
    far[1] = after(far[1], *sums, inverse)
    [other] = partial([(ring // 2, far)], (got,), sums[1:])
    other = send(other, swap)
    [mine] = partial([(ring // 2, far)], (hidden,), sums[:1])
    mixed = attend(lengths, learner, slot_offset, mine, other, inverse, *rotary())
    spread = exchange(mixed)
    landed = exchange(arrange(spread))
    return jnp.dot(slots(spread), landed, preferred_element_type=f32).astype(bf16)


def solution(mesh):
    placed = (
        P(("dp", "fsdp"), None),
        P(("dp", "fsdp")),
        P(("dp", "fsdp")),
        P(("dp", "fsdp")),
        P("fsdp"),
        P("fsdp", None),
        P("fsdp", None),
    )
    return jax.shard_map(
        shards, mesh=mesh, in_specs=placed, out_specs=P(("dp", "fsdp"), None), check_vma=False
    )
```

```python
import functools

import jax
import jax.numpy as jnp
import numpy as np
from jax import lax
from jax.experimental import pallas as pl
from jax.experimental.pallas import tpu as pltpu
from jax.sharding import PartitionSpec as P

HD = 128
QH = 4
WIDE = (QH + 2) * HD
PAIR = 128
TABLE = 128

rope_base = 500000.0
norm_eps = 1e-05

f32 = jnp.float32
bf16 = jnp.bfloat16


VMEM = pl.BlockSpec(memory_space=pltpu.VMEM)
SMEM = pl.BlockSpec(memory_space=pltpu.SMEM)


def fold_kernel(gain_ref, query_ref, keyval_ref, *out_refs):
    rows = out_refs[0].shape[0]
    row = lax.broadcasted_iota(jnp.int32, (rows, rows), 0)
    column = lax.broadcasted_iota(jnp.int32, (rows, rows), 1)
    for i, out_ref in enumerate(out_refs):
        own = slice(i * rows, (i + 1) * rows)
        gain = gain_ref[own].astype(f32).reshape(1, rows)
        gain = jnp.where(row == column, gain, 0.0).astype(bf16)
        query = jnp.dot(gain, query_ref[own, :], preferred_element_type=f32)
        keyval = jnp.dot(gain, keyval_ref[own, :], preferred_element_type=f32)
        out_ref[:, : QH * HD] = query.astype(bf16)
        out_ref[:, QH * HD :] = keyval.astype(bf16)


def fold(gain, query_weight, keyval_weight):
    half = jax.ShapeDtypeStruct((gain.shape[0] // 2, WIDE), bf16)
    return pl.pallas_call(
        fold_kernel,
        out_shape=[half] * 2,
        in_specs=[VMEM] * 3,
        out_specs=[VMEM] * 2,
        compiler_params=pltpu.CompilerParams(vmem_limit_bytes=16 << 20),
        name="fold_gain",
    )(gain, query_weight, keyval_weight)


def inverse_kernel(rows_ref, inverse_ref):
    tokens, depth = rows_ref.shape
    chunk = 4 * HD

    def add(i, total):
        rows = rows_ref[:, pl.ds(pl.multiple_of(i * chunk, chunk), chunk)]
        for j in range(0, chunk, HD):
            total += jnp.square(rows[:, j : j + HD].astype(f32))
        return total

    total = lax.fori_loop(0, depth // chunk, add, jnp.zeros((tokens, HD), f32))
    mean = jnp.sum(total, axis=1, keepdims=True) / depth
    inverse_ref[...] = jnp.broadcast_to(lax.rsqrt(mean + norm_eps), inverse_ref.shape)


def inverses(rows):
    tokens, depth = rows.shape
    return pl.pallas_call(
        inverse_kernel,
        out_shape=jax.ShapeDtypeStruct((tokens, HD), f32),
        in_specs=[VMEM],
        out_specs=VMEM,
        compiler_params=pltpu.CompilerParams(vmem_limit_bytes=24 << 20),
        cost_estimate=pl.CostEstimate(
            flops=2 * tokens * depth, bytes_accessed=2 * tokens * depth, transcendentals=0
        ),
        name="inverse",
    )(rows)


def partial_kernel(distances, sides, carried, *refs):
    count = len(distances)
    halves, refs = refs[: 2 * count], refs[2 * count :]
    rows, refs = refs[:sides], refs[sides:]
    before, refs = refs[: sides * carried], refs[sides * carried :]
    out_refs, (columns, arrived) = refs[:sides], refs[sides:]
    half = halves[0].shape[0]
    index = lax.axis_index("fsdp")
    place, core = lax.div(index, 2), lax.rem(index, 2)
    ring = lax.axis_size("fsdp") // 2
    copies = []
    for side in range(sides):
        for i, distance in enumerate(distances):
            origin = lax.rem(place + (ring + distance), ring)
            start = pl.multiple_of((2 * origin + core) * (2 * half), 2 * half)
            at = side * count + i
            copies.append(
                pltpu.make_async_copy(
                    rows[side].at[:, pl.ds(start, 2 * half)], columns.at[at], arrived.at[at]
                )
            )
            copies[-1].start()
    for side in range(sides):
        total = before[side][...] if carried else None
        for i in range(count):
            at = side * count + i
            copies[at].wait()
            for h in range(2):
                part = jnp.dot(
                    columns[at, :, h * half : (h + 1) * half],
                    halves[2 * i + h][...],
                    preferred_element_type=f32,
                )
                total = part if total is None else total + part
        out_refs[side][...] = total


def partial(blocks, rows, before):
    count, sides = len(blocks), len(rows)
    halves = [w for _, pair in blocks for w in pair]
    tokens, depth = rows[0].shape[0], 2 * halves[0].shape[0]
    carried = before is not None
    operands = [*halves, *rows, *(before or [])]
    return pl.pallas_call(
        functools.partial(partial_kernel, [d for d, _ in blocks], sides, carried),
        out_shape=[jax.ShapeDtypeStruct((tokens, WIDE), f32)] * sides,
        in_specs=[VMEM] * len(halves)
        + [pl.BlockSpec(memory_space=pl.ANY)] * sides
        + [VMEM] * (sides * carried),
        out_specs=[VMEM] * sides,
        scratch_shapes=[
            pltpu.VMEM((sides * count, tokens, depth), bf16),
            pltpu.SemaphoreType.DMA((sides * count,)),
        ],
        compiler_params=pltpu.CompilerParams(vmem_limit_bytes=28 << 20),
        cost_estimate=pl.CostEstimate(
            flops=2 * tokens * depth * WIDE * count * sides,
            bytes_accessed=2 * depth * (sides * tokens + WIDE) * count + 8 * tokens * WIDE * sides,
            transcendentals=0,
        ),
        name="partial_sums",
    )(*operands)


def attend_kernel(
    lengths_ref, learner_ref, offset_ref, mine_ref, other_ref, inverse_ref, cosine_ref, sine_ref, out_ref, mixed
):
    tokens = out_ref.shape[0]
    inverse = inverse_ref[...]

    def by_position(table_ref):
        table = table_ref[...]
        place = lax.broadcasted_iota(jnp.int32, table.shape, 0)
        leads = [lengths_ref[2 * k] for k in range(tokens // PAIR)]
        pairs = [jnp.where(place < n, table, pltpu.roll(table, n, 0)) for n in leads]
        return jnp.concatenate(pairs, axis=0) * inverse

    cosine, sine = by_position(cosine_ref), by_position(sine_ref)

    def product(head):
        own = slice(head * HD, (head + 1) * HD)
        return mine_ref[:, own] + other_ref[:, own]

    def rotated(head):
        values = product(head)
        return (values * cosine + pltpu.roll(values, HD // 2, 1) * sine).astype(bf16)

    heads = [rotated(h) for h in range(QH)]
    key_part = rotated(QH)
    value_part = (product(QH + 1) * inverse).astype(bf16)
    asks = lax.broadcasted_iota(jnp.int32, (PAIR, PAIR), 0)
    keys = lax.broadcasted_iota(jnp.int32, (PAIR, PAIR), 1)
    for pair in range(tokens // PAIR):
        own = slice(pair * PAIR, (pair + 1) * PAIR)
        lead = lengths_ref[2 * pair]
        allowed = (keys <= asks) & ((asks < lead) | (keys >= lead))
        barred = jnp.concatenate([jnp.where(allowed, 0.0, -1e30)] * QH, axis=0)
        query = jnp.concatenate([h[own] for h in heads], axis=0)
        scores = lax.dot_general(
            query, key_part[own], (((1,), (1,)), ((), ())), preferred_element_type=f32
        ) * (HD**-0.5)
        scores += barred
        weights = jnp.exp(scores - jnp.max(scores, axis=1, keepdims=True))
        share = 1.0 / jnp.sum(weights, axis=1, keepdims=True)
        probability = (weights * share).astype(bf16)
        result = jnp.dot(probability, value_part[own], preferred_element_type=f32).astype(bf16)
        for h in range(QH):
            mixed[own, h * HD : (h + 1) * HD] = result[h * PAIR : (h + 1) * PAIR]
    row = lax.broadcasted_iota(jnp.int32, (tokens, tokens), 0)
    token = lax.broadcasted_iota(jnp.int32, (tokens, tokens), 1)
    source = ((row >> 2) & 1) * PAIR + (row >> 3) * 4 + (row & 3)
    order = jnp.where(token == source, 1.0, 0.0).astype(bf16)
    out_ref[:, : QH * HD] = jnp.dot(order, mixed[...], preferred_element_type=f32).astype(bf16)
    lane = lax.broadcasted_iota(jnp.int32, (tokens, TABLE), 1)
    table = jnp.zeros((tokens, TABLE), jnp.int32)
    for i, ref in enumerate((lengths_ref, learner_ref, offset_ref)):
        for j in range(4):
            table = jnp.where(lane == 4 * i + j, ref[j], table)
    out_ref[:, QH * HD :] = table.astype(f32).astype(bf16)


def attend(lengths, learner, slot_offset, mine, other, inverse, cosine, sine):
    tokens = mine.shape[0]
    return pl.pallas_call(
        attend_kernel,
        out_shape=jax.ShapeDtypeStruct((tokens, QH * HD + TABLE), bf16),
        in_specs=[SMEM] * 3 + [VMEM] * 5,
        out_specs=VMEM,
        scratch_shapes=[pltpu.VMEM((tokens, QH * HD), bf16)],
        compiler_params=pltpu.CompilerParams(vmem_limit_bytes=16 << 20),
        name="attend",
    )(lengths, learner, slot_offset, mine, other, inverse, cosine, sine)


def rotary():
    lane = np.arange(HD)
    frequency = rope_base ** (-(lane % (HD // 2)) * 2.0 / HD)
    angles = np.arange(PAIR)[:, None] * frequency[None, :]
    sine = np.where(lane < HD // 2, -1.0, 1.0) * np.sin(angles)
    return np.cos(angles).astype(np.float32), sine.astype(np.float32)


def ranks(spread_ref):
    rows = spread_ref.shape[0]
    place = lax.broadcasted_iota(jnp.int32, (rows, 1), 0)
    table = spread_ref[:, QH * HD :].astype(f32)
    target = jnp.where((place >> 2) & 1 == 1, table[:, 6:7], table[:, 4:5])
    key = target * rows + (place >> 2).astype(f32)
    down = lax.broadcasted_iota(jnp.int32, (rows, rows), 0)
    along = lax.broadcasted_iota(jnp.int32, (rows, rows), 1)
    key_along = jnp.sum(jnp.where(down == along, key, 0.0), axis=0, keepdims=True)
    ahead_along = jnp.sum(jnp.where(key < key_along, 1.0, 0.0), axis=0, keepdims=True)
    return table, place, key, key_along, ahead_along.astype(jnp.int32), down


def arrange_kernel(spread_ref, out_ref):
    *_, ahead_along, down = ranks(spread_ref)
    row = lax.broadcasted_iota(jnp.int32, ahead_along.shape, 1)
    order = jnp.where(down == ahead_along + (row & 3), 1.0, 0.0).astype(bf16)
    out_ref[...] = jnp.dot(order, spread_ref[:, : QH * HD], preferred_element_type=f32).astype(bf16)


def slots_kernel(me_ref, spread_ref, out_ref):
    table, place, key, key_along, _, down = ranks(spread_ref)
    ahead = jnp.sum(jnp.where(key_along < key, 1.0, 0.0), axis=1, keepdims=True).astype(jnp.int32)
    second = (place >> 2) & 1 == 1
    row = lax.broadcasted_iota(jnp.int32, key_along.shape, 1)
    token = (row >> 3) * 4 + (row & 3)

    def slots(k):
        mine = (ahead == 4 * (2 * me_ref[0] + k)) & (place & 3 == 0)

        def own(even, odd):
            values = jnp.where(second, table[:, odd : odd + 1], table[:, even : even + 1])
            return jnp.sum(jnp.where(mine, values, 0.0), axis=0, keepdims=True).astype(jnp.int32)

        lead = own(0, 2)
        return jnp.where(token < lead, own(8, 10) + token, own(9, 11) + token - lead)

    slot = jnp.where((row >> 2) & 1 == 0, slots(0), slots(1))
    out_ref[...] = jnp.where(down == slot, 1.0, 0.0).astype(bf16)


def arrange(spread):
    return pl.pallas_call(
        arrange_kernel,
        out_shape=jax.ShapeDtypeStruct((spread.shape[0], QH * HD), bf16),
        in_specs=[VMEM],
        out_specs=VMEM,
        compiler_params=pltpu.CompilerParams(vmem_limit_bytes=16 << 20),
        name="arrange",
    )(spread)


def slots(spread):
    return pl.pallas_call(
        slots_kernel,
        out_shape=jax.ShapeDtypeStruct((spread.shape[0],) * 2, bf16),
        in_specs=[SMEM, VMEM],
        out_specs=VMEM,
        compiler_params=pltpu.CompilerParams(vmem_limit_bytes=16 << 20),
        name="slots",
    )(lax.axis_index("dp").reshape(1), spread)


def exchange(rows):
    blocks = rows.reshape(lax.axis_size("dp"), -1, rows.shape[1])
    return lax.all_to_all(blocks, "dp", split_axis=0, concat_axis=0, tiled=True).reshape(rows.shape)


def shards(hidden, lengths, learner, slot_offset, norm_gain, query_weight, keyval_weight):
    tokens = hidden.shape[0]
    size = lax.axis_size("fsdp")
    ring = size // 2
    up = [(i, (i + 2) % size) for i in range(size)]
    down = [(i, (i - 2) % size) for i in range(size)]
    swap = [(i, i ^ 1) for i in range(size)]

    def send(values, pairs):
        return lax.ppermute(values, "fsdp", pairs)

    def after(value, *others):
        return lax.optimization_barrier((value, *others))[0]

    held = fold(norm_gain, query_weight, keyval_weight)
    got = send(hidden, swap)
    both = (hidden, got)
    above, below = list(held), list(held)
    for step in range(1, ring // 2):
        near = (above, below)
        above = [send(w, up) for w in above]
        below = [send(w, down) for w in below]
        if step == 1:
            sums = partial([(0, (held[0], after(held[1], above[0])))], both, None)
            inverse = inverses(after(hidden, above[0]))
            above[1] = after(above[1], *sums, inverse)
        else:
            blocks = [(1 - step, near[0]), (step - 1, near[1])]
            sums = partial(blocks, both, sums)
            if step == 2:
                above[1] = after(above[1], *sums)
    far = [send(above[0], up), send(below[1], down)]
    last = step
    sums = partial([(-last, (above[0], after(above[1], *sums))), (last, below)], both, sums)
    far[1] = after(far[1], *sums)
    [other] = partial([(ring // 2, far)], (got,), sums[1:])
    other = send(other, swap)
    [mine] = partial([(ring // 2, far)], (hidden,), sums[:1])
    mixed = attend(lengths, learner, slot_offset, mine, other, inverse, *rotary())
    spread = exchange(mixed)
    landed = exchange(arrange(spread))
    return jnp.dot(slots(spread), landed, preferred_element_type=f32).astype(bf16)


def solution(mesh):
    placed = (
        P(("dp", "fsdp"), None),
        P(("dp", "fsdp")),
        P(("dp", "fsdp")),
        P(("dp", "fsdp")),
        P("fsdp"),
        P("fsdp", None),
        P("fsdp", None),
    )
    return jax.shard_map(
        shards, mesh=mesh, in_specs=placed, out_specs=P(("dp", "fsdp"), None), check_vma=False
    )
```

```python
import functools

import jax
import jax.numpy as jnp
import numpy as np
from jax import lax
from jax.experimental import pallas as pl
from jax.experimental.pallas import tpu as pltpu
from jax.sharding import PartitionSpec as P

HD = 128
QH = 4
WIDE = (QH + 2) * HD
PAIR = 128
TABLE = 128

rope_base = 500000.0
norm_eps = 1e-05

f32 = jnp.float32
bf16 = jnp.bfloat16


VMEM = pl.BlockSpec(memory_space=pltpu.VMEM)
SMEM = pl.BlockSpec(memory_space=pltpu.SMEM)


def fold_kernel(gain_hbm, query_hbm, keyval_hbm, *refs):
    (*outs_hbm, gain_ref, query_ref, keyval_ref, folded, arrived, left) = refs
    copies = [
        pltpu.make_async_copy(source, target, arrived.at[i])
        for i, (source, target) in enumerate(
            zip((gain_hbm, query_hbm, keyval_hbm), (gain_ref, query_ref, keyval_ref))
        )
    ]
    for copy in copies:
        copy.start()
    for copy in copies:
        copy.wait()
    rows = folded.shape[1]
    row = lax.broadcasted_iota(jnp.int32, (rows, rows), 0)
    column = lax.broadcasted_iota(jnp.int32, (rows, rows), 1)
    copies = []
    for i, out_hbm in enumerate(outs_hbm):
        own = slice(i * rows, (i + 1) * rows)
        gain = gain_ref[own].astype(f32).reshape(1, rows)
        gain = jnp.where(row == column, gain, 0.0).astype(bf16)
        query = jnp.dot(gain, query_ref[own, :], preferred_element_type=f32)
        keyval = jnp.dot(gain, keyval_ref[own, :], preferred_element_type=f32)
        folded[i, :, : QH * HD] = query.astype(bf16)
        folded[i, :, QH * HD :] = keyval.astype(bf16)
        copies.append(pltpu.make_async_copy(folded.at[i], out_hbm, left.at[i]))
        copies[-1].start()
    for copy in copies:
        copy.wait()


def fold(gain, query_weight, keyval_weight):
    depth = gain.shape[0]
    half = jax.ShapeDtypeStruct((depth // 2, WIDE), bf16)
    anywhere = pl.BlockSpec(memory_space=pl.ANY)
    return pl.pallas_call(
        fold_kernel,
        out_shape=[half] * 2,
        in_specs=[anywhere] * 3,
        out_specs=[anywhere] * 2,
        scratch_shapes=[
            pltpu.VMEM(gain.shape, bf16),
            pltpu.VMEM(query_weight.shape, bf16),
            pltpu.VMEM(keyval_weight.shape, bf16),
            pltpu.VMEM((2, depth // 2, WIDE), bf16),
            pltpu.SemaphoreType.DMA((3,)),
            pltpu.SemaphoreType.DMA((2,)),
        ],
        compiler_params=pltpu.CompilerParams(vmem_limit_bytes=60 << 20),
        name="fold_gain",
    )(gain, query_weight, keyval_weight)


def inverse_kernel(rows_ref, inverse_ref):
    tokens, depth = rows_ref.shape
    chunk = 4 * HD

    def add(i, total):
        rows = rows_ref[:, pl.ds(pl.multiple_of(i * chunk, chunk), chunk)]
        for j in range(0, chunk, HD):
            total += jnp.square(rows[:, j : j + HD].astype(f32))
        return total

    total = lax.fori_loop(0, depth // chunk, add, jnp.zeros((tokens, HD), f32))
    mean = jnp.sum(total, axis=1, keepdims=True) / depth
    inverse_ref[...] = jnp.broadcast_to(lax.rsqrt(mean + norm_eps), inverse_ref.shape)


def inverses(rows):
    tokens, depth = rows.shape
    return pl.pallas_call(
        inverse_kernel,
        out_shape=jax.ShapeDtypeStruct((tokens, HD), f32),
        in_specs=[VMEM],
        out_specs=VMEM,
        compiler_params=pltpu.CompilerParams(vmem_limit_bytes=24 << 20),
        cost_estimate=pl.CostEstimate(
            flops=2 * tokens * depth, bytes_accessed=2 * tokens * depth, transcendentals=0
        ),
        name="inverse",
    )(rows)


def partial_kernel(distances, sides, carried, *refs):
    count = len(distances)
    halves, refs = refs[: 2 * count], refs[2 * count :]
    rows, refs = refs[:sides], refs[sides:]
    before, refs = refs[: sides * carried], refs[sides * carried :]
    out_refs, (columns, arrived) = refs[:sides], refs[sides:]
    half = halves[0].shape[0]
    index = lax.axis_index("fsdp")
    place, core = lax.div(index, 2), lax.rem(index, 2)
    ring = lax.axis_size("fsdp") // 2
    copies = []
    for side in range(sides):
        for i, distance in enumerate(distances):
            origin = lax.rem(place + (ring + distance), ring)
            start = pl.multiple_of((2 * origin + core) * (2 * half), 2 * half)
            at = side * count + i
            copies.append(
                pltpu.make_async_copy(
                    rows[side].at[:, pl.ds(start, 2 * half)], columns.at[at], arrived.at[at]
                )
            )
            copies[-1].start()
    for side in range(sides):
        total = before[side][...] if carried else None
        for i in range(count):
            at = side * count + i
            copies[at].wait()
            for h in range(2):
                part = jnp.dot(
                    columns[at, :, h * half : (h + 1) * half],
                    halves[2 * i + h][...],
                    preferred_element_type=f32,
                )
                total = part if total is None else total + part
        out_refs[side][...] = total


def partial(blocks, rows, before):
    count, sides = len(blocks), len(rows)
    halves = [w for _, pair in blocks for w in pair]
    tokens, depth = rows[0].shape[0], 2 * halves[0].shape[0]
    carried = before is not None
    operands = [*halves, *rows, *(before or [])]
    return pl.pallas_call(
        functools.partial(partial_kernel, [d for d, _ in blocks], sides, carried),
        out_shape=[jax.ShapeDtypeStruct((tokens, WIDE), f32)] * sides,
        in_specs=[VMEM] * len(halves)
        + [pl.BlockSpec(memory_space=pl.ANY)] * sides
        + [VMEM] * (sides * carried),
        out_specs=[VMEM] * sides,
        scratch_shapes=[
            pltpu.VMEM((sides * count, tokens, depth), bf16),
            pltpu.SemaphoreType.DMA((sides * count,)),
        ],
        compiler_params=pltpu.CompilerParams(vmem_limit_bytes=28 << 20),
        cost_estimate=pl.CostEstimate(
            flops=2 * tokens * depth * WIDE * count * sides,
            bytes_accessed=2 * depth * (sides * tokens + WIDE) * count + 8 * tokens * WIDE * sides,
            transcendentals=0,
        ),
        name="partial_sums",
    )(*operands)


def attend_kernel(
    lengths_ref, learner_ref, offset_ref, mine_ref, other_ref, inverse_ref, cosine_ref, sine_ref, out_ref, mixed
):
    tokens = out_ref.shape[0]
    inverse = inverse_ref[...]

    def by_position(table_ref):
        table = table_ref[...]
        place = lax.broadcasted_iota(jnp.int32, table.shape, 0)
        leads = [lengths_ref[2 * k] for k in range(tokens // PAIR)]
        pairs = [jnp.where(place < n, table, pltpu.roll(table, n, 0)) for n in leads]
        return jnp.concatenate(pairs, axis=0) * inverse

    cosine, sine = by_position(cosine_ref), by_position(sine_ref)

    def product(head):
        own = slice(head * HD, (head + 1) * HD)
        return mine_ref[:, own] + other_ref[:, own]

    def rotated(head):
        values = product(head)
        return (values * cosine + pltpu.roll(values, HD // 2, 1) * sine).astype(bf16)

    heads = [rotated(h) for h in range(QH)]
    key_part = rotated(QH)
    value_part = (product(QH + 1) * inverse).astype(bf16)
    asks = lax.broadcasted_iota(jnp.int32, (PAIR, PAIR), 0)
    keys = lax.broadcasted_iota(jnp.int32, (PAIR, PAIR), 1)
    for pair in range(tokens // PAIR):
        own = slice(pair * PAIR, (pair + 1) * PAIR)
        lead = lengths_ref[2 * pair]
        allowed = (keys <= asks) & ((asks < lead) | (keys >= lead))
        barred = jnp.concatenate([jnp.where(allowed, 0.0, -1e30)] * QH, axis=0)
        query = jnp.concatenate([h[own] for h in heads], axis=0)
        scores = lax.dot_general(
            query, key_part[own], (((1,), (1,)), ((), ())), preferred_element_type=f32
        ) * (HD**-0.5)
        scores += barred
        weights = jnp.exp(scores - jnp.max(scores, axis=1, keepdims=True))
        share = 1.0 / jnp.sum(weights, axis=1, keepdims=True)
        probability = (weights * share).astype(bf16)
        result = jnp.dot(probability, value_part[own], preferred_element_type=f32).astype(bf16)
        for h in range(QH):
            mixed[own, h * HD : (h + 1) * HD] = result[h * PAIR : (h + 1) * PAIR]
    row = lax.broadcasted_iota(jnp.int32, (tokens, tokens), 0)
    token = lax.broadcasted_iota(jnp.int32, (tokens, tokens), 1)
    source = ((row >> 2) & 1) * PAIR + (row >> 3) * 4 + (row & 3)
    order = jnp.where(token == source, 1.0, 0.0).astype(bf16)
    out_ref[:, : QH * HD] = jnp.dot(order, mixed[...], preferred_element_type=f32).astype(bf16)
    lane = lax.broadcasted_iota(jnp.int32, (tokens, TABLE), 1)
    table = jnp.zeros((tokens, TABLE), jnp.int32)
    for i, ref in enumerate((lengths_ref, learner_ref, offset_ref)):
        for j in range(4):
            table = jnp.where(lane == 4 * i + j, ref[j], table)
    out_ref[:, QH * HD :] = table.astype(f32).astype(bf16)


def attend(lengths, learner, slot_offset, mine, other, inverse, cosine, sine):
    tokens = mine.shape[0]
    return pl.pallas_call(
        attend_kernel,
        out_shape=jax.ShapeDtypeStruct((tokens, QH * HD + TABLE), bf16),
        in_specs=[SMEM] * 3 + [VMEM] * 5,
        out_specs=VMEM,
        scratch_shapes=[pltpu.VMEM((tokens, QH * HD), bf16)],
        compiler_params=pltpu.CompilerParams(vmem_limit_bytes=16 << 20),
        name="attend",
    )(lengths, learner, slot_offset, mine, other, inverse, cosine, sine)


def rotary():
    lane = np.arange(HD)
    frequency = rope_base ** (-(lane % (HD // 2)) * 2.0 / HD)
    angles = np.arange(PAIR)[:, None] * frequency[None, :]
    sine = np.where(lane < HD // 2, -1.0, 1.0) * np.sin(angles)
    return np.cos(angles).astype(np.float32), sine.astype(np.float32)


def ranks(spread_ref):
    rows = spread_ref.shape[0]
    place = lax.broadcasted_iota(jnp.int32, (rows, 1), 0)
    table = spread_ref[:, QH * HD :].astype(f32)
    target = jnp.where((place >> 2) & 1 == 1, table[:, 6:7], table[:, 4:5])
    key = target * rows + (place >> 2).astype(f32)
    down = lax.broadcasted_iota(jnp.int32, (rows, rows), 0)
    along = lax.broadcasted_iota(jnp.int32, (rows, rows), 1)
    key_along = jnp.sum(jnp.where(down == along, key, 0.0), axis=0, keepdims=True)
    ahead_along = jnp.sum(jnp.where(key < key_along, 1.0, 0.0), axis=0, keepdims=True)
    return table, place, key, key_along, ahead_along.astype(jnp.int32), down


def arrange_kernel(spread_ref, out_ref):
    *_, ahead_along, down = ranks(spread_ref)
    row = lax.broadcasted_iota(jnp.int32, ahead_along.shape, 1)
    order = jnp.where(down == ahead_along + (row & 3), 1.0, 0.0).astype(bf16)
    out_ref[...] = jnp.dot(order, spread_ref[:, : QH * HD], preferred_element_type=f32).astype(bf16)


def slots_kernel(me_ref, spread_ref, out_ref):
    table, place, key, key_along, _, down = ranks(spread_ref)
    ahead = jnp.sum(jnp.where(key_along < key, 1.0, 0.0), axis=1, keepdims=True).astype(jnp.int32)
    second = (place >> 2) & 1 == 1
    row = lax.broadcasted_iota(jnp.int32, key_along.shape, 1)
    token = (row >> 3) * 4 + (row & 3)

    def slots(k):
        mine = (ahead == 4 * (2 * me_ref[0] + k)) & (place & 3 == 0)

        def own(even, odd):
            values = jnp.where(second, table[:, odd : odd + 1], table[:, even : even + 1])
            return jnp.sum(jnp.where(mine, values, 0.0), axis=0, keepdims=True).astype(jnp.int32)

        lead = own(0, 2)
        return jnp.where(token < lead, own(8, 10) + token, own(9, 11) + token - lead)

    slot = jnp.where((row >> 2) & 1 == 0, slots(0), slots(1))
    out_ref[...] = jnp.where(down == slot, 1.0, 0.0).astype(bf16)


def arrange(spread):
    return pl.pallas_call(
        arrange_kernel,
        out_shape=jax.ShapeDtypeStruct((spread.shape[0], QH * HD), bf16),
        in_specs=[VMEM],
        out_specs=VMEM,
        compiler_params=pltpu.CompilerParams(vmem_limit_bytes=16 << 20),
        name="arrange",
    )(spread)


def slots(spread):
    return pl.pallas_call(
        slots_kernel,
        out_shape=jax.ShapeDtypeStruct((spread.shape[0],) * 2, bf16),
        in_specs=[SMEM, VMEM],
        out_specs=VMEM,
        compiler_params=pltpu.CompilerParams(vmem_limit_bytes=16 << 20),
        name="slots",
    )(lax.axis_index("dp").reshape(1), spread)


def exchange(rows):
    blocks = rows.reshape(lax.axis_size("dp"), -1, rows.shape[1])
    return lax.all_to_all(blocks, "dp", split_axis=0, concat_axis=0, tiled=True).reshape(rows.shape)


def shards(hidden, lengths, learner, slot_offset, norm_gain, query_weight, keyval_weight):
    tokens = hidden.shape[0]
    size = lax.axis_size("fsdp")
    ring = size // 2
    up = [(i, (i + 2) % size) for i in range(size)]
    down = [(i, (i - 2) % size) for i in range(size)]
    swap = [(i, i ^ 1) for i in range(size)]

    def send(values, pairs):
        return lax.ppermute(values, "fsdp", pairs)

    def after(value, *others):
        return lax.optimization_barrier((value, *others))[0]

    held = fold(norm_gain, query_weight, keyval_weight)
    both = (hidden, send(hidden, swap))
    above, below = list(held), list(held)
    sums = None
    for step in range(1, ring // 2):
        near = (above, below)
        above = [send(w, up) for w in above]
        below = [send(w, down) for w in below]
        if step == 1:
            inverse = inverses(after(hidden, above[0]))
            above[1] = after(above[1], inverse)
        else:
            blocks = [(1 - step, near[0]), (step - 1, near[1])]
            sums = partial(blocks, both, sums)
            if step == 2:
                above[1] = after(above[1], *sums)
    far = [send(above[0], up), send(below[1], down)]
    blocks = [(-step, (above[0], after(above[1], *sums))), (step, below), (0, held)]
    sums = partial(blocks, both, sums)
    far[1] = after(far[1], *sums)
    [other] = partial([(ring // 2, far)], both[1:], sums[1:])
    other = send(other, swap)
    [mine] = partial([(ring // 2, far)], both[:1], sums[:1])
    mixed = attend(lengths, learner, slot_offset, mine, other, inverse, *rotary())
    spread = exchange(mixed)
    landed = exchange(arrange(spread))
    return jnp.dot(slots(spread), landed, preferred_element_type=f32).astype(bf16)


def solution(mesh):
    placed = (
        P(("dp", "fsdp"), None),
        P(("dp", "fsdp")),
        P(("dp", "fsdp")),
        P(("dp", "fsdp")),
        P("fsdp"),
        P("fsdp", None),
        P("fsdp", None),
    )
    return jax.shard_map(
        shards, mesh=mesh, in_specs=placed, out_specs=P(("dp", "fsdp"), None), check_vma=False
    )
```

```python
import functools

import jax
import jax.numpy as jnp
import numpy as np
from jax import lax
from jax.experimental import pallas as pl
from jax.experimental.pallas import tpu as pltpu
from jax.sharding import PartitionSpec as P

HD = 128
QH = 4
WIDE = (QH + 2) * HD
PAIR = 128
TABLE = 128

rope_base = 500000.0
norm_eps = 1e-05

f32 = jnp.float32
bf16 = jnp.bfloat16


VMEM = pl.BlockSpec(memory_space=pltpu.VMEM)
SMEM = pl.BlockSpec(memory_space=pltpu.SMEM)


def fold_kernel(gain_ref, query_ref, keyval_ref, *out_refs):
    rows = out_refs[0].shape[0]
    row = lax.broadcasted_iota(jnp.int32, (rows, rows), 0)
    column = lax.broadcasted_iota(jnp.int32, (rows, rows), 1)
    for i, out_ref in enumerate(out_refs):
        own = slice(i * rows, (i + 1) * rows)
        gain = gain_ref[own].astype(f32).reshape(1, rows)
        gain = jnp.where(row == column, gain, 0.0).astype(bf16)
        query = jnp.dot(gain, query_ref[own, :], preferred_element_type=f32)
        keyval = jnp.dot(gain, keyval_ref[own, :], preferred_element_type=f32)
        out_ref[:, : QH * HD] = query.astype(bf16)
        out_ref[:, QH * HD :] = keyval.astype(bf16)


def fold(gain, query_weight, keyval_weight):
    half = jax.ShapeDtypeStruct((gain.shape[0] // 2, WIDE), bf16)
    return pl.pallas_call(
        fold_kernel,
        out_shape=[half] * 2,
        in_specs=[VMEM] * 3,
        out_specs=[VMEM] * 2,
        compiler_params=pltpu.CompilerParams(vmem_limit_bytes=16 << 20),
        name="fold_gain",
    )(gain, query_weight, keyval_weight)


def inverse_kernel(rows_ref, inverse_ref):
    tokens, depth = rows_ref.shape
    chunk = 4 * HD

    def add(i, total):
        rows = rows_ref[:, pl.ds(pl.multiple_of(i * chunk, chunk), chunk)]
        for j in range(0, chunk, HD):
            total += jnp.square(rows[:, j : j + HD].astype(f32))
        return total

    total = lax.fori_loop(0, depth // chunk, add, jnp.zeros((tokens, HD), f32))
    mean = jnp.sum(total, axis=1, keepdims=True) / depth
    inverse_ref[...] = jnp.broadcast_to(lax.rsqrt(mean + norm_eps), inverse_ref.shape)


def inverses(rows):
    tokens, depth = rows.shape
    return pl.pallas_call(
        inverse_kernel,
        out_shape=jax.ShapeDtypeStruct((tokens, HD), f32),
        in_specs=[VMEM],
        out_specs=VMEM,
        compiler_params=pltpu.CompilerParams(vmem_limit_bytes=24 << 20),
        cost_estimate=pl.CostEstimate(
            flops=2 * tokens * depth, bytes_accessed=2 * tokens * depth, transcendentals=0
        ),
        name="inverse",
    )(rows)


def partial_kernel(distances, sides, carried, *refs):
    count = len(distances)
    halves, refs = refs[: 2 * count], refs[2 * count :]
    rows, refs = refs[:sides], refs[sides:]
    before, refs = refs[: sides * carried], refs[sides * carried :]
    out_refs, (columns, arrived) = refs[:sides], refs[sides:]
    half = halves[0].shape[0]
    index = lax.axis_index("fsdp")
    place, core = lax.div(index, 2), lax.rem(index, 2)
    ring = lax.axis_size("fsdp") // 2
    copies = []
    for side in range(sides):
        for i, distance in enumerate(distances):
            origin = lax.rem(place + (ring + distance), ring)
            start = pl.multiple_of((2 * origin + core) * (2 * half), 2 * half)
            at = side * count + i
            copies.append(
                pltpu.make_async_copy(
                    rows[side].at[:, pl.ds(start, 2 * half)], columns.at[at], arrived.at[at]
                )
            )
            copies[-1].start()
    for side in range(sides):
        total = before[side][...] if carried else None
        for i in range(count):
            at = side * count + i
            copies[at].wait()
            for h in range(2):
                part = jnp.dot(
                    columns[at, :, h * half : (h + 1) * half],
                    halves[2 * i + h][...],
                    preferred_element_type=f32,
                )
                total = part if total is None else total + part
        out_refs[side][...] = total.astype(out_refs[side].dtype)


def partial(blocks, rows, before, kind=f32):
    count, sides = len(blocks), len(rows)
    halves = [w for _, pair in blocks for w in pair]
    tokens, depth = rows[0].shape[0], 2 * halves[0].shape[0]
    carried = before is not None
    operands = [*halves, *rows, *(before or [])]
    return pl.pallas_call(
        functools.partial(partial_kernel, [d for d, _ in blocks], sides, carried),
        out_shape=[jax.ShapeDtypeStruct((tokens, WIDE), kind)] * sides,
        in_specs=[VMEM] * len(halves)
        + [pl.BlockSpec(memory_space=pl.ANY)] * sides
        + [VMEM] * (sides * carried),
        out_specs=[VMEM] * sides,
        scratch_shapes=[
            pltpu.VMEM((sides * count, tokens, depth), bf16),
            pltpu.SemaphoreType.DMA((sides * count,)),
        ],
        compiler_params=pltpu.CompilerParams(vmem_limit_bytes=28 << 20),
        cost_estimate=pl.CostEstimate(
            flops=2 * tokens * depth * WIDE * count * sides,
            bytes_accessed=2 * depth * (sides * tokens + WIDE) * count + 8 * tokens * WIDE * sides,
            transcendentals=0,
        ),
        name="partial_sums",
    )(*operands)


def attend_kernel(
    lengths_ref, learner_ref, offset_ref, mine_ref, other_ref, inverse_ref, cosine_ref, sine_ref, out_ref, mixed
):
    tokens = out_ref.shape[0]
    inverse = inverse_ref[...]

    def by_position(table_ref):
        table = table_ref[...]
        place = lax.broadcasted_iota(jnp.int32, table.shape, 0)
        leads = [lengths_ref[2 * k] for k in range(tokens // PAIR)]
        pairs = [jnp.where(place < n, table, pltpu.roll(table, n, 0)) for n in leads]
        return jnp.concatenate(pairs, axis=0) * inverse

    cosine, sine = by_position(cosine_ref), by_position(sine_ref)

    def product(head):
        own = slice(head * HD, (head + 1) * HD)
        return mine_ref[:, own] + other_ref[:, own].astype(f32)

    def rotated(head):
        values = product(head)
        return (values * cosine + pltpu.roll(values, HD // 2, 1) * sine).astype(bf16)

    heads = [rotated(h) for h in range(QH)]
    key_part = rotated(QH)
    value_part = (product(QH + 1) * inverse).astype(bf16)
    asks = lax.broadcasted_iota(jnp.int32, (PAIR, PAIR), 0)
    keys = lax.broadcasted_iota(jnp.int32, (PAIR, PAIR), 1)
    for pair in range(tokens // PAIR):
        own = slice(pair * PAIR, (pair + 1) * PAIR)
        lead = lengths_ref[2 * pair]
        allowed = (keys <= asks) & ((asks < lead) | (keys >= lead))
        barred = jnp.concatenate([jnp.where(allowed, 0.0, -1e30)] * QH, axis=0)
        query = jnp.concatenate([h[own] for h in heads], axis=0)
        scores = lax.dot_general(
            query, key_part[own], (((1,), (1,)), ((), ())), preferred_element_type=f32
        ) * (HD**-0.5)
        scores += barred
        weights = jnp.exp(scores - jnp.max(scores, axis=1, keepdims=True))
        share = 1.0 / jnp.sum(weights, axis=1, keepdims=True)
        probability = (weights * share).astype(bf16)
        result = jnp.dot(probability, value_part[own], preferred_element_type=f32).astype(bf16)
        for h in range(QH):
            mixed[own, h * HD : (h + 1) * HD] = result[h * PAIR : (h + 1) * PAIR]
    row = lax.broadcasted_iota(jnp.int32, (tokens, tokens), 0)
    token = lax.broadcasted_iota(jnp.int32, (tokens, tokens), 1)
    source = ((row >> 2) & 1) * PAIR + (row >> 3) * 4 + (row & 3)
    order = jnp.where(token == source, 1.0, 0.0).astype(bf16)
    out_ref[:, : QH * HD] = jnp.dot(order, mixed[...], preferred_element_type=f32).astype(bf16)
    lane = lax.broadcasted_iota(jnp.int32, (tokens, TABLE), 1)
    table = jnp.zeros((tokens, TABLE), jnp.int32)
    for i, ref in enumerate((lengths_ref, learner_ref, offset_ref)):
        for j in range(4):
            table = jnp.where(lane == 4 * i + j, ref[j], table)
    out_ref[:, QH * HD :] = table.astype(f32).astype(bf16)


def attend(lengths, learner, slot_offset, mine, other, inverse, cosine, sine):
    tokens = mine.shape[0]
    return pl.pallas_call(
        attend_kernel,
        out_shape=jax.ShapeDtypeStruct((tokens, QH * HD + TABLE), bf16),
        in_specs=[SMEM] * 3 + [VMEM] * 5,
        out_specs=VMEM,
        scratch_shapes=[pltpu.VMEM((tokens, QH * HD), bf16)],
        compiler_params=pltpu.CompilerParams(vmem_limit_bytes=16 << 20),
        name="attend",
    )(lengths, learner, slot_offset, mine, other, inverse, cosine, sine)


def rotary():
    lane = np.arange(HD)
    frequency = rope_base ** (-(lane % (HD // 2)) * 2.0 / HD)
    angles = np.arange(PAIR)[:, None] * frequency[None, :]
    sine = np.where(lane < HD // 2, -1.0, 1.0) * np.sin(angles)
    return np.cos(angles).astype(np.float32), sine.astype(np.float32)


def ranks(spread_ref):
    rows = spread_ref.shape[0]
    place = lax.broadcasted_iota(jnp.int32, (rows, 1), 0)
    table = spread_ref[:, QH * HD :].astype(f32)
    target = jnp.where((place >> 2) & 1 == 1, table[:, 6:7], table[:, 4:5])
    key = target * rows + (place >> 2).astype(f32)
    down = lax.broadcasted_iota(jnp.int32, (rows, rows), 0)
    along = lax.broadcasted_iota(jnp.int32, (rows, rows), 1)
    key_along = jnp.sum(jnp.where(down == along, key, 0.0), axis=0, keepdims=True)
    ahead_along = jnp.sum(jnp.where(key < key_along, 1.0, 0.0), axis=0, keepdims=True)
    return table, place, key, key_along, ahead_along.astype(jnp.int32), down


def arrange_kernel(spread_ref, out_ref):
    *_, ahead_along, down = ranks(spread_ref)
    row = lax.broadcasted_iota(jnp.int32, ahead_along.shape, 1)
    order = jnp.where(down == ahead_along + (row & 3), 1.0, 0.0).astype(bf16)
    out_ref[...] = jnp.dot(order, spread_ref[:, : QH * HD], preferred_element_type=f32).astype(bf16)


def slots_kernel(me_ref, spread_ref, out_ref):
    table, place, key, key_along, _, down = ranks(spread_ref)
    ahead = jnp.sum(jnp.where(key_along < key, 1.0, 0.0), axis=1, keepdims=True).astype(jnp.int32)
    second = (place >> 2) & 1 == 1
    row = lax.broadcasted_iota(jnp.int32, key_along.shape, 1)
    token = (row >> 3) * 4 + (row & 3)

    def slots(k):
        mine = (ahead == 4 * (2 * me_ref[0] + k)) & (place & 3 == 0)

        def own(even, odd):
            values = jnp.where(second, table[:, odd : odd + 1], table[:, even : even + 1])
            return jnp.sum(jnp.where(mine, values, 0.0), axis=0, keepdims=True).astype(jnp.int32)

        lead = own(0, 2)
        return jnp.where(token < lead, own(8, 10) + token, own(9, 11) + token - lead)

    slot = jnp.where((row >> 2) & 1 == 0, slots(0), slots(1))
    out_ref[...] = jnp.where(down == slot, 1.0, 0.0).astype(bf16)


def arrange(spread):
    return pl.pallas_call(
        arrange_kernel,
        out_shape=jax.ShapeDtypeStruct((spread.shape[0], QH * HD), bf16),
        in_specs=[VMEM],
        out_specs=VMEM,
        compiler_params=pltpu.CompilerParams(vmem_limit_bytes=16 << 20),
        name="arrange",
    )(spread)


def slots(spread):
    return pl.pallas_call(
        slots_kernel,
        out_shape=jax.ShapeDtypeStruct((spread.shape[0],) * 2, bf16),
        in_specs=[SMEM, VMEM],
        out_specs=VMEM,
        compiler_params=pltpu.CompilerParams(vmem_limit_bytes=16 << 20),
        name="slots",
    )(lax.axis_index("dp").reshape(1), spread)


def exchange(rows):
    blocks = rows.reshape(lax.axis_size("dp"), -1, rows.shape[1])
    return lax.all_to_all(blocks, "dp", split_axis=0, concat_axis=0, tiled=True).reshape(rows.shape)


def shards(hidden, lengths, learner, slot_offset, norm_gain, query_weight, keyval_weight):
    tokens = hidden.shape[0]
    size = lax.axis_size("fsdp")
    ring = size // 2
    up = [(i, (i + 2) % size) for i in range(size)]
    down = [(i, (i - 2) % size) for i in range(size)]
    swap = [(i, i ^ 1) for i in range(size)]

    def send(values, pairs):
        return lax.ppermute(values, "fsdp", pairs)

    def after(value, *others):
        return lax.optimization_barrier((value, *others))[0]

    held = fold(norm_gain, query_weight, keyval_weight)
    got = send(hidden, swap)
    both = (hidden, got)
    above, below = list(held), list(held)
    for step in range(1, ring // 2):
        near = (above, below)
        above = [send(w, up) for w in above]
        below = [send(w, down) for w in below]
        if step == 1:
            sums = partial([(0, (held[0], after(held[1], above[0])))], both, None)
            inverse = inverses(after(hidden, above[0]))
            above[1] = after(above[1], *sums, inverse)
        else:
            blocks = [(1 - step, near[0]), (step - 1, near[1])]
            sums = partial(blocks, both, sums)
            if step == 2:
                above[1] = after(above[1], *sums)
    far = [send(above[0], up), send(below[1], down)]
    last = step
    sums = partial([(-last, (above[0], after(above[1], *sums))), (last, below)], both, sums)
    far[1] = after(far[1], *sums)
    [other] = partial([(ring // 2, far)], (got,), sums[1:], bf16)
    other = send(other, swap)
    [mine] = partial([(ring // 2, far)], (hidden,), sums[:1])
    mixed = attend(lengths, learner, slot_offset, mine, other, inverse, *rotary())
    spread = exchange(mixed)
    landed = exchange(arrange(spread))
    return jnp.dot(slots(spread), landed, preferred_element_type=f32).astype(bf16)


def solution(mesh):
    placed = (
        P(("dp", "fsdp"), None),
        P(("dp", "fsdp")),
        P(("dp", "fsdp")),
        P(("dp", "fsdp")),
        P("fsdp"),
        P("fsdp", None),
        P("fsdp", None),
    )
    return jax.shard_map(
        shards, mesh=mesh, in_specs=placed, out_specs=P(("dp", "fsdp"), None), check_vma=False
    )
```
